32 devices in a mesh: dp: 8 (over y, x, core), ctx: 4 (over z).
Axes of the slice: x: 2, y: 2, z: 4, core: 2. Of those that a mesh axis runs over, the one named last changes fastest.
Arguments:
- activations: bfloat16 [8, 512, 2048], P('dp', 'ctx'), may hold values from -6 to 6
- segment_ids: int32 [8, 512], P('dp'), may hold values from 0 to 3, never falling along the last dimension, each value on 1 to 256 neighbouring positions
- ln1_gain: bfloat16 [2048], P(('dp', 'ctx')), may hold values from 0.25 to 1.75
- ln1_bias: bfloat16 [2048], P(('dp', 'ctx')), may hold values from -3 to 3
- q_weight: bfloat16 [2048, 2048], P(('dp', 'ctx')), may hold values from -0.125 to 0.125
- q_bias: bfloat16 [2048], P(('dp', 'ctx')), may hold values from -3 to 3
- kv_weight: bfloat16 [2048, 256], P(('dp', 'ctx')), may hold values from -0.125 to 0.125
- v_bias: bfloat16 [128], P(('dp', 'ctx')), may hold values from -3 to 3
- out_weight: bfloat16 [2048, 2048], P(('dp', 'ctx')), may hold values from -1 to 1
- out_bias: bfloat16 [2048], P(('dp', 'ctx')), may hold values from -3 to 3
- ln2_gain: bfloat16 [2048], P(('dp', 'ctx')), may hold values from 0.25 to 1.75
- ln2_bias: bfloat16 [2048], P(('dp', 'ctx')), may hold values from -3 to 3
- up_weight: bfloat16 [2048, 8192], P(('dp', 'ctx')), may hold values from -0.125 to 0.125
- up_bias: bfloat16 [8192], P(('dp', 'ctx')), may hold values from -3 to 3
- down_weight: bfloat16 [8192, 2048], P(('dp', 'ctx')), may hold values from -0.0625 to 0.0625
- down_bias: bfloat16 [2048], P(('dp', 'ctx')), may hold values from -3 to 3
- cotangent: bfloat16 [8, 512, 2048], P('dp', 'ctx'), may hold values from -6 to 6
Outputs:
- output: bfloat16 [8, 512, 2048], P('dp', 'ctx')
- input_grad: bfloat16 [8, 512, 2048], P('dp', 'ctx')
- ln1_gain_grad: float32 [2048], P(('dp', 'ctx'))
- ln1_bias_grad: float32 [2048], P(('dp', 'ctx'))
- q_weight_grad: float32 [2048, 2048], P(('dp', 'ctx'))
- q_bias_grad: float32 [2048], P(('dp', 'ctx'))
- kv_weight_grad: float32 [2048, 256], P(('dp', 'ctx'))
- v_bias_grad: float32 [128], P(('dp', 'ctx'))
- out_weight_grad: float32 [2048, 2048], P(('dp', 'ctx'))
- out_bias_grad: float32 [2048], P(('dp', 'ctx'))
- ln2_gain_grad: float32 [2048], P(('dp', 'ctx'))
- ln2_bias_grad: float32 [2048], P(('dp', 'ctx'))
- up_weight_grad: float32 [2048, 8192], P(('dp', 'ctx'))
- up_bias_grad: float32 [8192], P(('dp', 'ctx'))
- down_weight_grad: float32 [8192, 2048], P(('dp', 'ctx'))
- down_bias_grad: float32 [2048], P(('dp', 'ctx'))
The draws below stay inside these ranges and needn't reach their ends.
Inputs may be any that keep to these rules, and one draw needn't show every extreme that they name: segment_ids of a row never fall; every one of the 4 documents of a row holds 1 to 256 tokens, and one holds exactly 256.
All inputs are finite; a program needn't handle non-finite values.
Results may differ from the reference program's by a relative error of at most 0.013.
Values may be sent and summed in bfloat16 or wider, within the bound.
No kernel may reach another device: no remote copies, remote signals or barrier semaphores. Data moves between devices by JAX's collectives and lax.ppermute only.
A program may use at most 320 MiB of HBM per device.

```python
import math
import jax
import jax.numpy as jnp
import numpy as np
from jax import lax

D = 2048
HEADS = 16
HD = 128
FF = 8192
SEGS = 4
ROW = 512
N_DP = 8


def steps_of(rng, dims, cuts, low, largest):
    def one(dim, parts):
        steps = jax.random.uniform(jax.random.fold_in(jax.random.fold_in(rng, 6), dim), (parts,), jnp.float32, low / len(cuts), largest / len(cuts))
        return jnp.repeat(jnp.exp(steps), dims[dim] // parts).reshape((-1,) + (1,) * (len(dims) - dim - 1))

    factor_of = one(*cuts[0])
    for cut in cuts[1:]:
        factor_of = factor_of * one(*cut)
    return factor_of


def length_profile(amount, total, reach, skew):
    loads = [(1 << 20) // math.isqrt(grade ** skew) + 1 for grade in range(2, amount + 1)]
    spare, counts = total - reach - (amount - 1), [1] * (amount - 1)
    while spare > 0:
        free = [i for i in range(amount - 1) if counts[i] < reach]
        pool, remaining = sum([loads[i] for i in free]), spare
        for i in free:
            extra = min(reach - counts[i], max(1, remaining * loads[i] // pool), spare)
            counts[i] = counts[i] + extra
            spare = spare - extra
    return np.array([reach] + counts)


def uneven_parts(own_key, amount, total, bound, lean):
    if amount == 2:
        one = jax.random.randint(own_key, (), max(1, total - bound), min(bound, total - 1) + 1)
        return jnp.stack([one, total - one])
    sizes = jnp.asarray(length_profile(amount, total, bound, lean), jnp.int32)
    couples = (amount - 1) // 2
    donor, receiver = sizes[1:1 + 2 * couples:2], sizes[2:2 + 2 * couples:2]
    room = jnp.minimum(donor - 1, bound - receiver)
    shifted = jax.random.randint(jax.random.fold_in(own_key, 1), (couples,), 0, 1 << 20) % (room + 1)
    sizes = sizes.at[1:1 + 2 * couples:2].set(donor - shifted).at[2:2 + 2 * couples:2].set(receiver + shifted)
    return sizes[jax.random.permutation(jax.random.fold_in(own_key, 2), amount)]


def bell_draw(key, extent, deviation, limit, cuts=(), kind=jnp.bfloat16):
    level = steps_of(key, extent, cuts, -0.22, 0.18) if cuts else 1.0
    array = jax.random.normal(key, extent, jnp.float32) * deviation * level
    return jnp.minimum(jnp.maximum(array, -limit), limit).astype(kind)


def setup_inputs(seed: int = 0) -> dict:
    streams_of = jax.random.split(jax.random.key(seed), 18)
    return {
        "activations": bell_draw(streams_of[0], (N_DP, ROW, D), 1.0, 6.0, ((0, 8), (1, 4))),
        "segment_ids": jax.vmap(lambda own: jnp.searchsorted(jnp.cumsum(uneven_parts(own, SEGS, ROW, ROW // 2, 2)), jnp.arange(ROW), side="right"))(jax.random.split(streams_of[1], N_DP)).reshape((N_DP, ROW)).astype(jnp.int32),
        "ln1_gain": jnp.clip(1.0 + 0.15 * jax.random.normal(streams_of[2], (D,), jnp.float32), 0.25, 1.75).astype(jnp.bfloat16),
        "ln1_bias": bell_draw(streams_of[3], (D,), 0.3, 3.0, ((0, 32),)),
        "q_weight": bell_draw(streams_of[4], (D, D), D ** -0.5, 0.125, ((0, 32),)),
        "q_bias": bell_draw(streams_of[5], (D,), 0.3, 3.0, ((0, 32),)),
        "kv_weight": bell_draw(streams_of[6], (D, 2 * HD), D ** -0.5, 0.125, ((0, 32),)),
        "v_bias": bell_draw(streams_of[7], (HD,), 0.3, 3.0, ((0, 32),)),
        "out_weight": bell_draw(streams_of[8], (D, D), (D // 64) ** -0.5, 1.0, ((0, 32),)),
        "out_bias": bell_draw(streams_of[9], (D,), 0.3, 3.0, ((0, 32),)),
        "ln2_gain": jnp.clip(1.0 + 0.15 * jax.random.normal(streams_of[10], (D,), jnp.float32), 0.25, 1.75).astype(jnp.bfloat16),
        "ln2_bias": bell_draw(streams_of[11], (D,), 0.3, 3.0, ((0, 32),)),
        "up_weight": bell_draw(streams_of[12], (D, FF), D ** -0.5, 0.125, ((0, 32),)),
        "up_bias": bell_draw(streams_of[13], (FF,), 0.3, 3.0, ((0, 32),)),
        "down_weight": bell_draw(streams_of[14], (FF, D), FF ** -0.5, 0.0625, ((0, 32),)),
        "down_bias": bell_draw(streams_of[15], (D,), 0.3, 3.0, ((0, 32),)),
        "cotangent": bell_draw(streams_of[16], (N_DP, ROW, D), 1.0, 6.0, ((0, 8), (1, 4))),
    }


epsilon = 1e-05
highest = lax.Precision.HIGHEST

@jax.custom_vjp
def low(v):
    return lax.optimization_barrier(v.astype(jnp.bfloat16)).astype(jnp.float32)

@jax.custom_vjp
def low_back(v):
    return v

def low_keep(v):
    return (low(v), None)

def low_pass(kept, grad):
    return (grad,)

def back_keep(v):
    return (v, None)

def back_low(kept, grad):
    return (low(grad),)
low.defvjp(low_keep, low_pass)
low_back.defvjp(back_keep, back_low)

def norm_rows(values, gain, shift):
    center = lax.optimization_barrier(jnp.mean(values, axis=-1, keepdims=True))
    centered = values - center
    variance = lax.optimization_barrier(jnp.mean(centered * centered, axis=-1, keepdims=True))
    return centered * lax.rsqrt(variance + epsilon) * gain + shift

def layer_row(row_values, row_segments, params):
    gain_one, shift_one, weight_query, bias_query, weight_kv, bias_value, weight_out, bias_out, gain_two, shift_two, weight_up, bias_up, weight_down, bias_down = params
    length = row_values.shape[0]
    hidden_one = low(norm_rows(row_values, gain_one, shift_one))
    queries = jnp.dot(hidden_one, weight_query, precision=highest) + bias_query
    queries = low_back(low(queries))
    kv_shift = jnp.concatenate([jnp.zeros((HD,), jnp.float32), bias_value])
    key_value = jnp.dot(hidden_one, weight_kv, precision=highest) + kv_shift
    key_value = low_back(low(key_value))
    key_rows = key_value[:, :HD]
    value_rows = key_value[:, HD:]
    query_heads = queries.reshape(length, HEADS, HD)
    scores = jnp.einsum('thd,jd->htj', query_heads, key_rows, precision=highest) * HD ** (-0.5)
    scores = low_back(scores)
    places = jnp.arange(length, dtype=jnp.int32)
    allowed = (places[None, :] <= places[:, None]) & (row_segments[None, :] == row_segments[:, None])
    scores = jnp.where(allowed[None], scores, -1e+30)
    biggest = lax.optimization_barrier(jnp.max(scores, axis=-1, keepdims=True))
    expons = jnp.exp(scores - biggest)
    soft_rows = low(expons / lax.optimization_barrier(jnp.sum(expons, axis=-1, keepdims=True)))
    attended = jnp.einsum('htj,jd->thd', soft_rows, value_rows, precision=highest).reshape(length, HEADS * HD)
    attended = low_back(low(attended))
    branch = low_back(jnp.dot(attended, weight_out, precision=highest) + bias_out)
    middle = row_values + branch
    hidden_two = low(norm_rows(middle, gain_two, shift_two))
    preact = low_back(jnp.dot(hidden_two, weight_up, precision=highest) + bias_up)
    activ = low(jax.nn.gelu(preact, approximate=True))
    mlp_out = low_back(jnp.dot(activ, weight_down, precision=highest) + bias_down)
    return middle + mlp_out

def reference(activations, segment_ids, ln1_gain, ln1_bias, q_weight, q_bias, kv_weight, v_bias, out_weight, out_bias, ln2_gain, ln2_bias, up_weight, up_bias, down_weight, down_bias, cotangent):
    params = tuple((item.astype(jnp.float32) for item in (ln1_gain, ln1_bias, q_weight, q_bias, kv_weight, v_bias, out_weight, out_bias, ln2_gain, ln2_bias, up_weight, up_bias, down_weight, down_bias)))

    def one_row(totals, inputs):
        row_values, row_segments, row_cot = inputs

        def forward(values, weights):
            return layer_row(values, row_segments, weights)
        result, backward = jax.vjp(forward, row_values.astype(jnp.float32), params)
        grad_row, grad_params = backward(row_cot.astype(jnp.float32))
        totals = tuple((first + second for first, second in zip(totals, grad_params)))
        return (totals, (result.astype(jnp.bfloat16), grad_row.astype(jnp.bfloat16)))
    zeros = tuple((jnp.zeros(item.shape, jnp.float32) for item in params))
    totals, (results, grads) = lax.scan(one_row, zeros, (activations, segment_ids, cotangent))
    return (results, grads, totals[0], totals[1], totals[2], totals[3], totals[4], totals[5], totals[6], totals[7], totals[8], totals[9], totals[10], totals[11], totals[12], totals[13])
```

```python
import jax
import jax.numpy as jnp
from jax import lax
from jax.sharding import Mesh, PartitionSpec as P

HEADS = 16
HD = 128
EPS = 1e-05
GELU_K = 0.7978845608028654
GELU_C = 0.044715

BF = jnp.bfloat16
F32 = jnp.float32
CHIP = ("a", "b")
EVERY = ("a", "b", "core", "ctx")


def dot(a, b, dims):
    return lax.dot_general(a, b, (dims, ((), ())), preferred_element_type=F32)


def mm(a, b):
    return dot(a, b, ((1,), (0,)))


def mm_nt(a, b):
    return dot(a, b, ((1,), (1,)))


def mm_tn(a, b):
    return dot(a, b, ((0,), (0,)))


def ln_stats(x):
    mean = jnp.mean(x, axis=-1, keepdims=True)
    cen = x - mean
    var = jnp.mean(cen * cen, axis=-1, keepdims=True)
    rstd = lax.rsqrt(var + EPS)
    return cen * rstd, rstd


def ln_back(dh, gain, xhat, rstd):
    e = dh * gain
    me = jnp.mean(e, axis=-1, keepdims=True)
    mx = jnp.mean(e * xhat, axis=-1, keepdims=True)
    return (e - me - xhat * mx) * rstd


def make_local(A, B, Z):
    C = 2
    AB = A * B
    N = AB * C * Z
    mates = [(0, 1), (1, 0)]

    def swap_core(x):
        return lax.ppermute(x, "core", mates)

    def gather(x, axes, axis=0):
        return lax.all_gather(x, axes, axis=axis, tiled=False)

    def scatter(x, axes, axis=0):
        return lax.psum_scatter(x, axes, scatter_dimension=axis, tiled=False)

    def local(
        activations, segment_ids,
        ln1_gain, ln1_bias, q_weight, q_bias, kv_weight, v_bias, out_weight, out_bias,
        ln2_gain, ln2_bias, up_weight, up_bias, down_weight, down_bias, cotangent,
    ):
        T, D = activations.shape[1:]
        S = segment_ids.shape[1]
        R = q_weight.shape[0]
        F0 = down_weight.shape[0]
        F = AB * F0
        FF = up_weight.shape[1]
        DH = D // 2
        HH = HEADS // 2
        aligned = (Z * R) % HD == 0
        G = AB if aligned else 1
        W0 = DH // G
        c = lax.axis_index("core")
        z = lax.axis_index("ctx")

        vb0 = v_bias.shape[0]
        small = jnp.concatenate(
            [ln1_gain, ln1_bias, q_bias, out_bias, ln2_gain, ln2_bias, down_bias, up_bias, v_bias]
        )
        small = jnp.broadcast_to(small[None], (N, small.shape[0]))
        small = lax.all_to_all(small, EVERY, 0, 0, tiled=True).astype(F32)
        g1, b1, bq, bo, g2, b2, bd = (small[:, i * R : (i + 1) * R].reshape(D) for i in range(7))
        bu = small[:, 7 * R : 7 * R + F0].reshape(AB, C * Z, F0)
        bu = lax.dynamic_index_in_dim(bu, c * Z + z, 1, keepdims=False).reshape(F)
        bv = small[:, 7 * R + F0 :].reshape(HD)
        bq = lax.dynamic_index_in_dim(bq.reshape(G, 2, W0), c, 1, keepdims=False).reshape(DH)
        b_ext = jnp.concatenate([bq, jnp.where(c == 1, bv, 0.0)])

        w_ext = jnp.concatenate(
            [
                q_weight.reshape(R, G, 2, W0).transpose(2, 0, 1, 3).reshape(2, R, DH),
                kv_weight.reshape(R, 2, HD).transpose(1, 0, 2),
            ],
            axis=2,
        )
        E = DH + HD
        w_ext = lax.all_to_all(w_ext, "core", 0, 0, tiled=True)
        w_ext = gather(w_ext, "ctx", axis=1)
        w_ext = gather(w_ext, CHIP).reshape(D, E)
        if aligned:
            w_out = gather(gather(out_weight, "ctx"), CHIP).reshape(DH, D)
        else:
            w_out = gather(out_weight, EVERY).reshape(2, DH, D)
            w_out = lax.dynamic_index_in_dim(w_out, c, 0, keepdims=False)

        w_up = up_weight.reshape(R, AB, C * Z, F0).transpose(2, 0, 1, 3).reshape(C * Z, R, F)
        w_up = lax.all_to_all(w_up, ("core", "ctx"), 0, 0, tiled=True)
        w_up = gather(w_up, CHIP).reshape(D, F)
        w_down = gather(down_weight, CHIP).reshape(F, D)

        cot = cotangent[0]
        cot_z = gather(cot, "ctx")
        cot_all = jnp.stack([cot_z, swap_core(cot_z)]).reshape(2 * Z * T, D)

        x = activations[0].astype(F32)
        xhat1, rstd1 = ln_stats(x)
        h1 = (xhat1 * g1 + b1).astype(BF)
        h1 = jnp.concatenate([h1, swap_core(h1)])
        q_ext = (mm(h1, w_ext) + b_ext).astype(BF)
        q = q_ext[:, :DH].reshape(2, T, HH, HD)
        kv = gather(q_ext[:, DH:].reshape(2, T, HD), "ctx", axis=1).reshape(2, S, HD)
        kv_mate = swap_core(kv)[::-1]
        k = jnp.where(c == 0, kv, kv_mate)
        v = jnp.where(c == 0, kv_mate, kv)
        seg = jnp.concatenate([segment_ids, swap_core(segment_ids)])
        start = z * T
        seg_q = lax.dynamic_slice_in_dim(seg, start, T, axis=1)
        q_at = start + jnp.arange(T, dtype=jnp.int32)
        k_at = jnp.arange(S, dtype=jnp.int32)
        allowed = (k_at[None, None, :] <= q_at[None, :, None]) & (seg[:, None, :] == seg_q[:, :, None])
        s = jnp.einsum("rthd,rjd->rhtj", q, k, preferred_element_type=F32) * HD**-0.5
        s = jnp.where(allowed[:, None], s, -1e30)
        p = jnp.exp(s - jnp.max(s, axis=-1, keepdims=True))
        p = p / jnp.sum(p, axis=-1, keepdims=True)
        pb = p.astype(BF)
        o = jnp.einsum("rhtj,rjd->rthd", pb, v, preferred_element_type=F32)
        o = o.astype(BF).reshape(2 * T, DH)
        part = mm(o, w_out)
        mid = x + bo + part[:T] + swap_core(part[T:])

        xhat2, rstd2 = ln_stats(mid)
        h2 = (xhat2 * g2 + b2).astype(BF)
        h2_z = gather(h2, "ctx")
        h2_all = jnp.stack([h2_z, swap_core(h2_z)]).reshape(2 * Z * T, D)
        pre = mm(h2_all, w_up) + bu
        th = jnp.tanh(GELU_K * (pre + GELU_C * pre * pre * pre))
        act = (0.5 * pre * (1.0 + th)).astype(BF)
        dgelu = 0.5 * (1.0 + th) + 0.5 * pre * (1.0 - th * th) * GELU_K * (1.0 + 3.0 * GELU_C * pre * pre)

        def token_sum(part):
            half = Z * T
            mine = part[:half] + swap_core(part[half:].astype(BF)).astype(F32)
            return scatter(mine.reshape(Z, T, D).astype(BF), "ctx").astype(F32)

        dact = mm_nt(cot_all, w_down)
        dpre = (dact * dgelu).astype(BF)
        dh2 = token_sum(mm_nt(dpre, w_up))
        result = mid + token_sum(mm(act, w_down)) + bd
        g_down = scatter(mm_tn(act, cot_all).astype(BF).reshape(AB, F0, D), CHIP).astype(F32)
        g_up = scatter(mm_tn(h2_all, dpre).astype(BF).reshape(AB, C * Z, R, F), CHIP)
        g_up = lax.all_to_all(g_up, ("core", "ctx"), 0, 0, tiled=True)
        g_up = g_up.reshape(C * Z, R, AB, F0).transpose(1, 2, 0, 3).reshape(R, FF).astype(F32)
        gb_up = jnp.sum(dpre.astype(F32), axis=0)

        cot32 = cot.astype(F32)
        dmid = cot32 + ln_back(dh2, g2, xhat2, rstd2)
        db_own = dmid.astype(BF)
        db = jnp.concatenate([db_own, swap_core(db_own)])
        g_out = mm_tn(o, db).astype(BF)
        if aligned:
            g_out = scatter(scatter(g_out.reshape(AB, Z, R, D), CHIP), "ctx").astype(F32)
        else:
            full = jnp.where(lax.broadcasted_iota(jnp.int32, (2, 1, 1), 0) == c, g_out[None], 0)
            g_out = scatter(full.reshape(N, R, D), EVERY).astype(F32)
        do = mm_nt(db, w_out).astype(BF).reshape(2, T, HH, HD)
        dp = jnp.einsum("rthd,rjd->rhtj", do, v, preferred_element_type=F32)
        ds = (p * (dp - jnp.sum(p * dp, axis=-1, keepdims=True))).astype(BF)
        dq = jnp.einsum("rhtj,rjd->rthd", ds, k, preferred_element_type=F32) * HD**-0.5
        dk = jnp.einsum("rhtj,rthd->rjd", ds, q, preferred_element_type=F32) * HD**-0.5
        dv = jnp.einsum("rhtj,rthd->rjd", pb, do, preferred_element_type=F32)
        away = jnp.where(c == 0, dv, dk).astype(BF)
        here = jnp.where(c == 0, dk, dv)
        here = here + swap_core(away)[::-1].astype(F32)
        dkv = here.astype(BF).reshape(2, Z, T, HD).transpose(1, 0, 2, 3)
        dkv = lax.all_to_all(dkv, "ctx", 0, 0, tiled=True)
        dkv = jnp.sum(dkv.astype(F32), axis=0).astype(BF).reshape(2 * T, HD)
        dq_ext = jnp.concatenate([dq.astype(BF).reshape(2 * T, DH), dkv], axis=1)
        part1 = mm_nt(dq_ext, w_ext)
        dh1 = part1[:T] + swap_core(part1[T:])
        g_ext = mm_tn(h1, dq_ext).astype(BF).reshape(AB, 2, Z, R, E)
        g_ext = scatter(scatter(g_ext, CHIP), "ctx", axis=1)
        g_ext = lax.all_to_all(g_ext, "core", 0, 0, tiled=True)
        g_q = g_ext[:, :, :DH].reshape(2, R, G, W0).transpose(1, 2, 0, 3).reshape(R, D).astype(F32)
        g_kv = g_ext[:, :, DH:].transpose(1, 0, 2).reshape(R, 2 * HD).astype(F32)
        gb_ext = jnp.sum(dq_ext.astype(F32), axis=0)
        dx = dmid + ln_back(dh1, g1, xhat1, rstd1)

        own_core = (lax.broadcasted_iota(jnp.int32, (1, 2, 1), 1) == c).astype(F32)
        own_cz = (lax.broadcasted_iota(jnp.int32, (1, C * Z, 1), 1) == c * Z + z).astype(F32)
        wide = [
            jnp.sum(dh1 * xhat1, axis=0),
            jnp.sum(dh1, axis=0),
            (gb_ext[:DH].reshape(G, 1, W0) * own_core).reshape(D),
            jnp.sum(db_own.astype(F32), axis=0),
            jnp.sum(dh2 * xhat2, axis=0),
            jnp.sum(dh2, axis=0),
            jnp.sum(cot32, axis=0),
        ]
        packed = jnp.concatenate(
            [w.reshape(N, R) for w in wide]
            + [
                (gb_up.reshape(AB, 1, F0) * own_cz).reshape(N, F0),
                jnp.where(c == 1, gb_ext[DH:], 0.0).reshape(N, vb0),
            ],
            axis=1,
        )
        packed = jnp.sum(lax.all_to_all(packed, EVERY, 0, 0, tiled=True), axis=0)
        v_ = [packed[i * R : (i + 1) * R] for i in range(7)]
        gb_up = packed[7 * R : 7 * R + F0]
        gb_v = packed[7 * R + F0 :]
        return (
            result.astype(BF)[None], dx.astype(BF)[None],
            v_[0], v_[1], g_q, v_[2], g_kv, gb_v, g_out, v_[3],
            v_[4], v_[5], g_up, gb_up, g_down, v_[6],
        )

    return local


def solution(mesh):
    dp, ctx = mesh.shape["dp"], mesh.shape["ctx"]
    chips = dp // 2
    a = next(i for i in range(int(chips**0.5), 0, -1) if chips % i == 0)
    b = chips // a
    fine = Mesh(mesh.devices.reshape(a, b, 2, ctx), EVERY)
    tok = P(("a", "b", "core"), "ctx", None)
    vec = P(EVERY)
    mat = P(EVERY, None)
    in_specs = (
        tok, P(("a", "b", "core"), None),
        vec, vec, mat, vec, mat, vec, mat, vec, vec, vec, mat, vec, mat, vec, tok,
    )
    out_specs = (tok, tok, vec, vec, mat, vec, mat, vec, mat, vec, vec, vec, mat, vec, mat, vec)
    return jax.shard_map(
        make_local(a, b, ctx), mesh=fine, in_specs=in_specs, out_specs=out_specs, check_vma=False
    )
```

```python
import jax
import jax.numpy as jnp
from jax import lax
from jax.sharding import Mesh, PartitionSpec as P

HEADS = 16
HD = 128
EPS = 1e-05
GELU_K = 0.7978845608028654
GELU_C = 0.044715

BF = jnp.bfloat16
F32 = jnp.float32
CHIP = ("a", "b")
EVERY = ("a", "b", "core", "ctx")
MATES = [(0, 1), (1, 0)]


def dot(a, b, dims):
    return lax.dot_general(a, b, (dims, ((), ())), preferred_element_type=F32)


def mm(a, b):
    return dot(a, b, ((1,), (0,)))


def mm_nt(a, b):
    return dot(a, b, ((1,), (1,)))


def mm_tn(a, b):
    return dot(a, b, ((0,), (0,)))


def ln_stats(x):
    mean = jnp.mean(x, axis=-1, keepdims=True)
    cen = x - mean
    var = jnp.mean(cen * cen, axis=-1, keepdims=True)
    rstd = lax.rsqrt(var + EPS)
    return cen * rstd, rstd


def ln_back(dh, gain, xhat, rstd):
    e = dh * gain
    me = jnp.mean(e, axis=-1, keepdims=True)
    mx = jnp.mean(e * xhat, axis=-1, keepdims=True)
    return (e - me - xhat * mx) * rstd


def after(x, *others):
    return lax.optimization_barrier((x, others))[0]


def swap_core(x):
    return lax.ppermute(x, "core", MATES)


def over_a(x):
    return lax.ppermute(x, "a", MATES)


def over_b(x):
    return lax.ppermute(x, "b", MATES)


def gather(x, axes):
    return lax.all_gather(x, axes, axis=0, tiled=False)


def scatter(x, axes):
    return lax.psum_scatter(x, axes, scatter_dimension=0, tiled=False)


class Order:
    def __init__(self):
        self.last = []

    def mark(self, *done):
        self.last = list(done)

    def __call__(self, *xs):
        xs = lax.optimization_barrier((xs, self.last))[0]
        return xs[0] if len(xs) == 1 else xs


class ChipGather:
    def __init__(self, x, square):
        self.square = square
        if not square:
            self.pieces = list(gather(x, CHIP).reshape((-1,) + x.shape))
            return
        self.pieces = [x, over_b(x), over_a(x)]

    def pass_on(self, order):
        if self.square:
            x, x1, x2 = self.pieces
            x1, x2 = order(x1, x2)
            half = x.shape[0] // 2
            self.pieces = [x, x1, x2, over_a(x1[:half]), over_b(x2[half:])]


class ChipSum:
    def __init__(self, term, square, count):
        self.square, self.term = square, term
        self.far = []
        if not square:
            full = jnp.stack([term((i, 0), (i, 1)) for i in range(count)])
            self.result = scatter(full.astype(BF), CHIP).astype(F32)
            self.sent = [full]
            return
        u = term((3, 0), (1, 0)).astype(BF)
        w = term((3, 1), (2, 1)).astype(BF)
        self.sent = [u, w]
        self.near = [over_b(u), over_a(w)]

    def pass_on(self, order):
        if self.square:
            u, w = self.near = order(*self.near)
            half = u.shape[0] // 2
            u = (self.term((2, 0)) + u[:half].astype(F32)).astype(BF)
            w = (self.term((1, 1)) + w[:half].astype(F32)).astype(BF)
            self.sent = [u, w]
            self.far = [over_a(u), over_b(w)]

    def finish(self, order):
        if not self.square:
            return self.result
        f0, f1 = order(*self.far)
        half = f0.shape[0]
        n0, n1 = self.near[0][half:], self.near[1][half:]
        return self.term((0, 0), (0, 1)) + (
            jnp.concatenate([n0, n1]).astype(F32) + jnp.concatenate([f0, f1]).astype(F32)
        )


def make_local(A, B, Z):
    C = 2
    AB = A * B
    N = AB * C * Z
    square = A == 2 and B == 2

    def turn(x, me):
        if not square:
            return x
        w = x.shape[1] // AB
        cols = [x[:, i * w : (i + 1) * w] for i in range(AB)]
        return jnp.concatenate([lax.select_n(me ^ i, *cols) for i in range(AB)], axis=1)

    def product(left, right):
        half = left.shape[1] // AB // 2
        return lambda *parts: mm_tn(
            jnp.concatenate([left[:, (2 * i + j) * half : (2 * i + j + 1) * half] for i, j in parts], axis=1), right
        )

    def local(
        activations, segment_ids,
        ln1_gain, ln1_bias, q_weight, q_bias, kv_weight, v_bias, out_weight, out_bias,
        ln2_gain, ln2_bias, up_weight, up_bias, down_weight, down_bias, cotangent,
    ):
        T, D = activations.shape[1:]
        S = segment_ids.shape[1]
        R = q_weight.shape[0]
        F0 = down_weight.shape[0]
        F = AB * F0
        FF = up_weight.shape[1]
        DH = D // 2
        HH = HEADS // 2
        aligned = (Z * R) % HD == 0
        G = AB if aligned else 1
        W0 = DH // G
        E = DH + HD
        c = lax.axis_index("core")
        z = lax.axis_index("ctx")
        me = lax.axis_index("a") * B + lax.axis_index("b")

        order = Order()

        def half_of(i):
            cols = [q_weight[:, (g * 2 + i) * W0 : (g * 2 + i + 1) * W0] for g in range(G)]
            return jnp.concatenate(cols + [kv_weight[:, i * HD : (i + 1) * HD]], axis=1)

        first, second = half_of(0), half_of(1)
        mine = jnp.where(c == 0, first, second)
        mate = swap_core(jnp.where(c == 0, second, first))
        w_ext = jnp.concatenate([jnp.where(c == 0, mine, mate), jnp.where(c == 0, mate, mine)])
        order.mark(w_ext)
        w_ext_z = gather(w_ext, "ctx").reshape(Z, 2, R, E).transpose(1, 0, 2, 3).reshape(2 * Z * R, E)

        down_gather = ChipGather(order(down_weight), square)
        order.mark(w_ext)
        small, xin = order(
            [ln1_gain, ln1_bias, q_bias, out_bias, ln2_gain, ln2_bias, down_bias, up_bias, v_bias], activations[0]
        )
        vb0 = v_bias.shape[0]
        small = jnp.concatenate(small)
        small = jnp.broadcast_to(small[None], (N, small.shape[0]))
        small = lax.all_to_all(small, EVERY, 0, 0, tiled=True).astype(F32)
        g1, b1, bq, bo, g2, b2, bd = (small[:, i * R : (i + 1) * R].reshape(D) for i in range(7))
        bu = small[:, 7 * R : 7 * R + F0].reshape(AB, C * Z, F0)
        bu = lax.dynamic_index_in_dim(bu, c * Z + z, 1, keepdims=False).reshape(F)
        bv = small[:, 7 * R + F0 :].reshape(HD)
        bq = lax.dynamic_index_in_dim(bq.reshape(G, 2, W0), c, 1, keepdims=False).reshape(DH)
        b_ext = jnp.concatenate([bq, jnp.where(c == 1, bv, 0.0)])
        x = xin.astype(F32)
        xhat1, rstd1 = ln_stats(x)
        h1 = turn((xhat1 * g1 + b1).astype(BF), me)
        h1 = jnp.concatenate([h1, swap_core(h1)])
        seg = jnp.concatenate([segment_ids, swap_core(segment_ids)])
        start = z * T
        seg_q = lax.dynamic_slice_in_dim(seg, start, T, axis=1)
        q_at = start + jnp.arange(T, dtype=jnp.int32)
        k_at = jnp.arange(S, dtype=jnp.int32)
        allowed = (k_at[None, None, :] <= q_at[None, :, None]) & (seg[:, None, :] == seg_q[:, :, None])
        order.mark(b_ext)
        down_gather.pass_on(order)
        order.mark(h1, down_gather.pieces[1:3])

        out_in = after(out_weight, w_ext_z)
        up_in = after(up_weight, w_ext_z)
        w_ext_z = order(w_ext_z)
        ext_gather = ChipGather(w_ext_z, square)
        if aligned:
            w_out_z = gather(out_in, "ctx").reshape(Z * R, D)
        else:
            w_out = gather(out_in, EVERY).reshape(2, DH, D)
            w_out = w_out_z = lax.dynamic_index_in_dim(w_out, c, 0, keepdims=False)
        up_cols = [
            jnp.concatenate([up_in[:, (i * C * Z + j) * F0 : (i * C * Z + j + 1) * F0] for i in range(AB)], axis=1)
            for j in range(C * Z)
        ]
        w_up = lax.all_to_all(jnp.stack(up_cols), ("core", "ctx"), 0, 0, tiled=True)
        ext_gather.pass_on(order)

        w_ext = jnp.concatenate(ext_gather.pieces)
        order.mark(w_ext)
        w_out_z, h1, w_up = order(w_out_z, h1, w_up)
        if aligned:
            out_gather = ChipGather(w_out_z, square)
        cot_z = gather(after(cotangent[0], w_out_z), "ctx").reshape(Z * T, D)
        q_ext = (mm(h1, w_ext) + b_ext).astype(BF)
        kv = gather(q_ext[:, DH:].reshape(2, T, HD), "ctx").transpose(1, 0, 2, 3).reshape(2, S, HD)
        q = q_ext[:, :DH]
        if aligned:
            q = turn(q, me)
        q = q.reshape(2, T, HH, HD)
        kv_mate = swap_core(kv)[::-1]
        k = jnp.where(c == 0, kv, kv_mate)
        v = jnp.where(c == 0, kv_mate, kv)
        order.mark(kv)
        q, k, cot_z = order(q, k, cot_z)
        s = jnp.einsum("rthd,rjd->rhtj", q, k, preferred_element_type=F32) * HD**-0.5
        s = jnp.where(allowed[:, None], s, -1e30)
        p = jnp.exp(s - jnp.max(s, axis=-1, keepdims=True))
        p = p / jnp.sum(p, axis=-1, keepdims=True)
        pb = p.astype(BF)
        o = jnp.einsum("rhtj,rjd->rthd", pb, v, preferred_element_type=F32)
        o = o.astype(BF).reshape(2 * T, DH)
        if aligned:
            order.mark(o)
            out_gather.pass_on(order)
            w_out = jnp.concatenate(out_gather.pieces)
        order.mark(w_out, cot_z)
        o_w, w_up_z = order(o, w_up.reshape(C * Z * R, F))
        up_gather = ChipGather(w_up_z, square)
        away = swap_core(mm(o_w[T:], w_out))
        mid = x + bo + mm(o_w[:T], w_out) + away

        xhat2, rstd2 = ln_stats(mid)
        h2 = turn((xhat2 * g2 + b2).astype(BF), me)
        h2_z = gather(h2, "ctx").reshape(Z * T, D)

        order.mark(h2)
        up_gather.pass_on(order)
        half = Z * T
        cot_z, down_pieces = order(cot_z, down_gather.pieces)
        cots = [cot_z, swap_core(cot_z)]
        if square:
            w_down = jnp.zeros((F, D), BF)
            places = [(0, 0), (1, 0), (2, 0), (3, 0), (3, 1)]
            for part, (block, j) in zip(down_pieces, places):
                at = (me ^ block) * F0 + j * (F0 // 2)
                w_down = lax.dynamic_update_slice_in_dim(w_down, part, at, 0)
        else:
            w_down = jnp.concatenate(down_pieces)
        dacts = [mm_nt(part, w_down) for part in cots]
        w_up = jnp.concatenate(up_gather.pieces)
        order.mark(dacts, w_up)
        h2_z = order(h2_z)
        h2s = [h2_z, swap_core(h2_z)]
        acts, dpres = [], []
        for part, dact in zip(h2s, dacts):
            pre = mm(part, w_up) + bu
            th = jnp.tanh(GELU_K * (pre + GELU_C * pre * pre * pre))
            slope = 1.0 - th * th
            dgelu = 0.5 * (1.0 + th) + 0.5 * pre * slope * GELU_K * (1.0 + 3.0 * GELU_C * pre * pre)
            acts.append((0.5 * pre * (1.0 + th)).astype(BF))
            dpres.append((dact * dgelu).astype(BF))
        away = swap_core(mm_nt(dpres[1], w_up).astype(BF))
        dh2_part = (mm_nt(after(dpres[0], away), w_up) + away.astype(F32)).astype(BF).reshape(Z, T, D)
        order.mark(dh2_part)
        dh2 = turn(scatter(dh2_part, "ctx").astype(F32), me)
        dpre_w, act_w, h2_all, cot_all = (jnp.concatenate(order(*pair)) for pair in (dpres, acts, h2s, cots))

        def down_term(*parts):
            half = F0 // 2
            cols = [
                lax.dynamic_slice_in_dim(act_w, (me ^ i if square else i) * F0 + j * half, half, axis=1)
                for i, j in parts
            ]
            return mm_tn(jnp.concatenate(cols, axis=1), cot_all)

        down_sum = ChipSum(down_term, square, AB)
        order.mark(down_sum.sent)
        up_sum = ChipSum(product(order(h2_all), dpre_w), square, AB)
        out_away = swap_core(mm(order(acts[1]), w_down).astype(BF))
        order.mark(up_sum.sent, out_away)
        down_sum.pass_on(order)
        order.mark(down_sum.sent)
        mlp = (mm(order(acts[0]), w_down) + out_away.astype(F32)).astype(BF).reshape(Z, T, D)
        order.mark(mlp)
        mlp = scatter(mlp, "ctx")

        dh2 = order(dh2)
        order.mark(dh2)
        dmid = cotangent[0].astype(F32) + ln_back(dh2, g2, xhat2, rstd2)
        db = dmid.astype(BF)
        db = jnp.concatenate([db, swap_core(db)])
        do = mm_nt(db, w_out).astype(BF)
        order.mark(do)
        do_h = order(do).reshape(2, T, HH, HD)
        dp = jnp.einsum("rthd,rjd->rhtj", do_h, v, preferred_element_type=F32)
        ds = (p * (dp - jnp.sum(p * dp, axis=-1, keepdims=True))).astype(BF)
        dk = jnp.einsum("rhtj,rthd->rjd", ds, q, preferred_element_type=F32) * HD**-0.5
        dv = jnp.einsum("rhtj,rthd->rjd", pb, do_h, preferred_element_type=F32)
        dkv_away = swap_core(jnp.where(c == 0, dv, dk).astype(BF))
        dkv = jnp.where(c == 0, dk, dv) + dkv_away[::-1].astype(F32)
        dkv = dkv.astype(BF).reshape(2, Z, T, HD).transpose(1, 0, 2, 3)
        order.mark(dkv, down_sum.far)
        dkv = lax.all_to_all(dkv, "ctx", 0, 0, tiled=True)
        up_sum.pass_on(order)
        order.mark(up_sum.sent)
        ds_w, db_w = order(ds, db)
        dq = jnp.einsum("rhtj,rjd->rthd", ds_w, k, preferred_element_type=F32) * HD**-0.5
        dq = dq.astype(BF).reshape(2 * T, DH)
        if aligned:
            dq = turn(dq, me)
            out_sum = ChipSum(product(o, db_w), square, AB)
            order.mark(out_sum.sent, dq)
        dkv = order(dkv)
        dkv = jnp.sum(dkv.astype(F32), axis=0).astype(BF).reshape(2 * T, HD)
        dq_ext = jnp.concatenate([dq, dkv], axis=1)
        ext_sum = ChipSum(product(h1, dq_ext), square, AB)
        order.mark(ext_sum.sent)
        g_up = up_sum.finish(order).astype(BF).reshape(C * Z, R, F)
        order.mark(g_up)
        g_up = lax.all_to_all(g_up, ("core", "ctx"), 0, 0, tiled=True)
        if aligned:
            out_sum.pass_on(order)
            order.mark(out_sum.sent)
        ext_sum.pass_on(order)
        order.mark(ext_sum.sent)
        dq_w = order(dq_ext)
        dh1_away = swap_core(mm_nt(dq_w[T:], w_ext))
        dh1 = turn(mm_nt(dq_w[:T], w_ext) + dh1_away, me)

        if aligned:
            g_out = out_sum.finish(order).astype(BF).reshape(Z, R, D)
            order.mark(g_out)
            g_out = lax.all_to_all(g_out, "ctx", 0, 0, tiled=True)
            g_out = jnp.sum(g_out.astype(F32), axis=0)
        else:
            g_out = mm_tn(o, order(db)).astype(BF)
            full = jnp.where(lax.broadcasted_iota(jnp.int32, (2, 1, 1), 0) == c, g_out[None], 0)
            g_out = scatter(full.reshape(N, R, D), EVERY).astype(F32)
        order.mark(ext_sum.far, g_up)
        g_ext = ext_sum.finish(order).astype(BF).reshape(2, Z, R, E)
        g_ext = g_ext.transpose(1, 0, 2, 3).reshape(Z, 2 * R, E)
        order.mark(g_ext)
        g_ext = scatter(g_ext, "ctx").reshape(2, R, E)
        g_down = down_sum.finish(order)
        dx = dmid + ln_back(order(dh1), g1, xhat1, rstd1)
        first, second = g_ext[0], g_ext[1]
        mate = swap_core(jnp.where(c == 0, second, first))
        mine = jnp.where(c == 0, first, second)
        first, second = jnp.where(c == 0, mine, mate), jnp.where(c == 0, mate, mine)
        g_q = [h[:, g * W0 : (g + 1) * W0] for g in range(G) for h in (first, second)]
        g_q = jnp.concatenate(g_q, axis=1).astype(F32)
        g_kv = jnp.concatenate([first[:, DH:], second[:, DH:]], axis=1).astype(F32)
        g_up = order(g_up)
        g_up = g_up.reshape(C * Z, R, AB, F0).transpose(1, 2, 0, 3).reshape(R, FF).astype(F32)
        result = mid + order(mlp).astype(F32) + bd

        own_core = (lax.broadcasted_iota(jnp.int32, (1, 2, 1), 1) == c).astype(F32)
        own_cz = (lax.broadcasted_iota(jnp.int32, (1, C * Z, 1), 1) == c * Z + z).astype(F32)
        dh2_late, dpre_late, cot_late, dq_late, db_late = order(dh2, dpre_w, cotangent[0], dq_ext, db[:T])
        gb_up = jnp.sum(dpre_late.astype(F32), axis=0)
        gb_ext = jnp.sum(dq_late.astype(F32), axis=0)
        wide = [
            jnp.sum(dh1 * xhat1, axis=0),
            jnp.sum(dh1, axis=0),
            (gb_ext[:DH].reshape(G, 1, W0) * own_core).reshape(D),
            jnp.sum(db_late.astype(F32), axis=0),
            jnp.sum(dh2_late * xhat2, axis=0),
            jnp.sum(dh2_late, axis=0),
            jnp.sum(cot_late.astype(F32), axis=0),
        ]
        packed = jnp.concatenate(
            [w.reshape(N, R) for w in wide]
            + [
                (gb_up.reshape(AB, 1, F0) * own_cz).reshape(N, F0),
                jnp.where(c == 1, gb_ext[DH:], 0.0).reshape(N, vb0),
            ],
            axis=1,
        )
        packed = jnp.sum(lax.all_to_all(packed, EVERY, 0, 0, tiled=True), axis=0)
        vecs = [packed[i * R : (i + 1) * R] for i in range(7)]
        gb_up = packed[7 * R : 7 * R + F0]
        gb_v = packed[7 * R + F0 :]
        return (
            result.astype(BF)[None], dx.astype(BF)[None],
            vecs[0], vecs[1], g_q, vecs[2], g_kv, gb_v, g_out, vecs[3],
            vecs[4], vecs[5], g_up, gb_up, g_down, vecs[6],
        )

    return local


def solution(mesh):
    dp, ctx = mesh.shape["dp"], mesh.shape["ctx"]
    chips = dp // 2
    a = next(i for i in range(int(chips**0.5), 0, -1) if chips % i == 0)
    b = chips // a
    fine = Mesh(mesh.devices.reshape(a, b, 2, ctx), EVERY)
    tok = P(("a", "b", "core"), "ctx", None)
    vec = P(EVERY)
    mat = P(EVERY, None)
    in_specs = (
        tok, P(("a", "b", "core"), None),
        vec, vec, mat, vec, mat, vec, mat, vec, vec, vec, mat, vec, mat, vec, tok,
    )
    out_specs = (tok, tok, vec, vec, mat, vec, mat, vec, mat, vec, vec, vec, mat, vec, mat, vec)
    return jax.shard_map(
        make_local(a, b, ctx), mesh=fine, in_specs=in_specs, out_specs=out_specs, check_vma=False
    )
```

```python
import jax
import jax.numpy as jnp
from jax import lax
from jax.experimental import pallas as pl
from jax.experimental.pallas import tpu as pltpu
from jax.sharding import Mesh, PartitionSpec as P

HEADS = 16
HD = 128
EPS = 1e-05
GELU_K = 0.7978845608028654
GELU_C = 0.044715

BF = jnp.bfloat16
F32 = jnp.float32
CHIP = ("a", "b")
EVERY = ("a", "b", "core", "ctx")
MATES = [(0, 1), (1, 0)]


def dot(a, b, dims):
    return lax.dot_general(a, b, (dims, ((), ())), preferred_element_type=F32)


def mm(a, b):
    return dot(a, b, ((1,), (0,)))


def mm_nt(a, b):
    return dot(a, b, ((1,), (1,)))


def mm_tn(a, b):
    return dot(a, b, ((0,), (0,)))


def side(a, b, ca, cb, out=F32):
    count, cols, depth = a.shape[1 - ca], b.shape[1 - cb], a.shape[ca]
    tile = next((t for t in (512, 384, 256, 128) if cols % t == 0), cols)

    def kernel(a_ref, b_ref, o_ref):
        o_ref[...] = lax.dot_general(
            a_ref[...], b_ref[...], (((ca,), (cb,)), ((), ())), preferred_element_type=F32
        ).astype(out)

    return pl.pallas_call(
        kernel,
        out_shape=jax.ShapeDtypeStruct((count, cols), out),
        grid=(cols // tile,),
        in_specs=[
            pl.BlockSpec(a.shape, lambda j: (0, 0)),
            pl.BlockSpec((depth, tile), lambda j: (0, j)) if cb == 0 else pl.BlockSpec((tile, depth), lambda j: (j, 0)),
        ],
        out_specs=pl.BlockSpec((count, tile), lambda j: (0, j)),
        compiler_params=pltpu.CompilerParams(vmem_limit_bytes=24 << 20),
        cost_estimate=pl.CostEstimate(flops=0, bytes_accessed=0, transcendentals=0),
        name="side",
    )(a, b)


def hidden(h, w_up, bias, dact):
    count, depth = h.shape
    units = w_up.shape[1]
    tile = next((t for t in (256, 128) if units % t == 0), units)

    def kernel(h_ref, w_ref, b_ref, d_ref, act_ref, dpre_ref):
        pre = jnp.dot(h_ref[...], w_ref[...], preferred_element_type=F32) + b_ref[...]
        square = pre * pre
        th = jnp.tanh(GELU_K * pre * (1.0 + GELU_C * square))
        half = 0.5 * (1.0 + th)
        act_ref[...] = (pre * half).astype(BF)
        slope = half + 0.5 * GELU_K * pre * (1.0 - th * th) * (1.0 + 3.0 * GELU_C * square)
        dpre_ref[...] = (d_ref[...] * slope).astype(BF)

    return pl.pallas_call(
        kernel,
        out_shape=[jax.ShapeDtypeStruct((count, units), BF)] * 2,
        grid=(units // tile,),
        in_specs=[
            pl.BlockSpec((count, depth), lambda j: (0, 0)),
            pl.BlockSpec((depth, tile), lambda j: (0, j)),
            pl.BlockSpec((1, tile), lambda j: (0, j)),
            pl.BlockSpec((count, tile), lambda j: (0, j)),
        ],
        out_specs=[pl.BlockSpec((count, tile), lambda j: (0, j))] * 2,
        compiler_params=pltpu.CompilerParams(vmem_limit_bytes=24 << 20),
        cost_estimate=pl.CostEstimate(
            flops=2 * count * depth * units, bytes_accessed=2 * (count + units) * depth, transcendentals=count * units
        ),
        name="hidden",
    )(h, w_up, bias.reshape(1, units), dact)


def ln_stats(x):
    mean = jnp.mean(x, axis=-1, keepdims=True)
    cen = x - mean
    var = jnp.mean(cen * cen, axis=-1, keepdims=True)
    rstd = lax.rsqrt(var + EPS)
    return cen * rstd, rstd


def ln_back(dh, gain, xhat, rstd):
    e = dh * gain
    me = jnp.mean(e, axis=-1, keepdims=True)
    mx = jnp.mean(e * xhat, axis=-1, keepdims=True)
    return (e - me - xhat * mx) * rstd


def after(x, *others):
    return lax.optimization_barrier((x, others))[0]


def swap_core(x):
    return lax.ppermute(x, "core", MATES)


def over_a(x):
    return lax.ppermute(x, "a", MATES)


def over_b(x):
    return lax.ppermute(x, "b", MATES)


def gather(x, axes):
    return lax.all_gather(x, axes, axis=0, tiled=False)


def scatter(x, axes):
    return lax.psum_scatter(x, axes, scatter_dimension=0, tiled=False)


class Order:
    def __init__(self):
        self.last = []

    def mark(self, *done):
        self.last = list(done)

    def __call__(self, *xs):
        xs = lax.optimization_barrier((xs, self.last))[0]
        return xs[0] if len(xs) == 1 else xs


class ChipGather:
    def __init__(self, x, square):
        self.square = square
        if not square:
            self.pieces = list(gather(x, CHIP).reshape((-1,) + x.shape))
            return
        self.pieces = [x, over_b(x), over_a(x)]

    def pass_on(self, *joint):
        if self.square:
            x, x1, x2 = self.pieces
            (x1, x2), joint = lax.optimization_barrier(((x1, x2), joint))
            half = x.shape[0] // 2
            self.pieces = [x, x1, x2, over_a(x1[:half]), over_b(x2[half:])]
        return joint


class ChipSum:
    def __init__(self, term, square, count, gate=()):
        self.square, self.term = square, term
        self.far = []
        if not square:
            full = jnp.stack([term((i, 0), (i, 1)) for i in range(count)])
            self.result = scatter(full.astype(BF), CHIP).astype(F32)
            self.sent = [full]
            return
        u = term((3, 0), (1, 0)).astype(BF)
        w = term((3, 1), (2, 1)).astype(BF)
        self.sent = [u, w]
        if gate:
            u, w = after((u, w), *gate)
        self.near = [over_b(u), over_a(w)]

    def pass_on(self, order):
        if self.square:
            u, w = self.near = order(*self.near)
            half = u.shape[0] // 2
            u = (self.term((2, 0)) + u[:half].astype(F32)).astype(BF)
            w = (self.term((1, 1)) + w[:half].astype(F32)).astype(BF)
            self.sent = [u, w]
            self.far = [over_a(u), over_b(w)]

    def finish(self, order):
        if not self.square:
            return self.result
        f0, f1 = order(*self.far)
        half = f0.shape[0]
        n0, n1 = self.near[0][half:], self.near[1][half:]
        return self.term((0, 0), (0, 1)) + (
            jnp.concatenate([n0, n1]).astype(F32) + jnp.concatenate([f0, f1]).astype(F32)
        )


def make_local(A, B, Z):
    C = 2
    AB = A * B
    N = AB * C * Z
    square = A == 2 and B == 2

    def turn(x, me):
        if not square:
            return x
        w = x.shape[1] // AB
        cols = [x[:, i * w : (i + 1) * w] for i in range(AB)]
        return jnp.concatenate([lax.select_n(me ^ i, *cols) for i in range(AB)], axis=1)

    def product(left, right, multiply=None):
        half = left.shape[1] // AB // 2

        def term(*parts):
            cols = [left[:, (2 * i + j) * half : (2 * i + j + 1) * half] for i, j in parts]
            cols = jnp.concatenate(cols, axis=1)
            return mm_tn(cols, right) if multiply is None else multiply(cols, right, 0, 0)

        return term

    def local(
        activations, segment_ids,
        ln1_gain, ln1_bias, q_weight, q_bias, kv_weight, v_bias, out_weight, out_bias,
        ln2_gain, ln2_bias, up_weight, up_bias, down_weight, down_bias, cotangent,
    ):
        T, D = activations.shape[1:]
        S = segment_ids.shape[1]
        R = q_weight.shape[0]
        F0 = down_weight.shape[0]
        F = AB * F0
        FF = up_weight.shape[1]
        DH = D // 2
        HH = HEADS // 2
        aligned = (Z * R) % HD == 0
        G = AB if aligned else 1
        W0 = DH // G
        E = DH + HD
        c = lax.axis_index("core")
        z = lax.axis_index("ctx")
        me = lax.axis_index("a") * B + lax.axis_index("b")

        order = Order()

        def half_of(i):
            cols = [q_weight[:, (g * 2 + i) * W0 : (g * 2 + i + 1) * W0] for g in range(G)]
            return jnp.concatenate(cols + [kv_weight[:, i * HD : (i + 1) * HD]], axis=1)

        first, second = half_of(0), half_of(1)
        mine = jnp.where(c == 0, first, second)
        mate = swap_core(jnp.where(c == 0, second, first))
        w_ext = jnp.concatenate([jnp.where(c == 0, mine, mate), jnp.where(c == 0, mate, mine)])
        order.mark(w_ext)
        w_ext_z = gather(w_ext, "ctx").reshape(Z, 2, R, E).transpose(1, 0, 2, 3).reshape(2 * Z * R, E)

        down_gather = ChipGather(order(down_weight), square)
        order.mark(w_ext)
        small, xin = order(
            [ln1_gain, ln1_bias, q_bias, out_bias, ln2_gain, ln2_bias, down_bias, up_bias, v_bias], activations[0]
        )
        vb0 = v_bias.shape[0]
        small = jnp.concatenate(small)
        small = jnp.broadcast_to(small[None], (N, small.shape[0]))
        small = lax.all_to_all(small, EVERY, 0, 0, tiled=True).astype(F32)
        g1, b1, bq, bo, g2, b2, bd = (small[:, i * R : (i + 1) * R].reshape(D) for i in range(7))
        bu = small[:, 7 * R : 7 * R + F0].reshape(AB, C * Z, F0)
        bu = lax.dynamic_index_in_dim(bu, c * Z + z, 1, keepdims=False).reshape(F)
        bv = small[:, 7 * R + F0 :].reshape(HD)
        bq = lax.dynamic_index_in_dim(bq.reshape(G, 2, W0), c, 1, keepdims=False).reshape(DH)
        b_ext = jnp.concatenate([bq, jnp.where(c == 1, bv, 0.0)])
        x = xin.astype(F32)
        xhat1, rstd1 = ln_stats(x)
        h1 = turn((xhat1 * g1 + b1).astype(BF), me)
        h1 = jnp.concatenate([h1, swap_core(h1)])
        seg = jnp.concatenate([segment_ids, swap_core(segment_ids)])
        start = z * T
        seg_q = lax.dynamic_slice_in_dim(seg, start, T, axis=1)
        q_at = start + jnp.arange(T, dtype=jnp.int32)
        k_at = jnp.arange(S, dtype=jnp.int32)
        allowed = (k_at[None, None, :] <= q_at[None, :, None]) & (seg[:, None, :] == seg_q[:, :, None])
        out_in = after(out_weight, w_ext_z)
        up_in = after(up_weight, w_ext_z)
        w_ext_z = order(w_ext_z)
        ext_gather = ChipGather(w_ext_z, square)
        if aligned:
            w_out_z = gather(out_in, "ctx").reshape(Z * R, D)
        else:
            w_out = gather(out_in, EVERY).reshape(2, DH, D)
            w_out = w_out_z = lax.dynamic_index_in_dim(w_out, c, 0, keepdims=False)
        up_cols = [
            jnp.concatenate([up_in[:, (i * C * Z + j) * F0 : (i * C * Z + j + 1) * F0] for i in range(AB)], axis=1)
            for j in range(C * Z)
        ]
        w_up = lax.all_to_all(jnp.stack(up_cols), ("core", "ctx"), 0, 0, tiled=True)
        w_out_z, down_gather.pieces = ext_gather.pass_on(w_out_z, down_gather.pieces)
        down_gather.pass_on()
        ext_gather.pieces, w_up = lax.optimization_barrier((ext_gather.pieces, w_up))

        w_ext = jnp.concatenate(ext_gather.pieces)
        order.mark(w_ext)
        h1 = order(h1)
        if aligned:
            out_gather = ChipGather(w_out_z, square)
        cot_z = gather(after(cotangent[0], w_out_z), "ctx").reshape(Z * T, D)
        q_ext = (mm(h1, w_ext) + b_ext).astype(BF)
        kv = gather(q_ext[:, DH:].reshape(2, T, HD), "ctx").transpose(1, 0, 2, 3).reshape(2, S, HD)
        q = q_ext[:, :DH]
        if aligned:
            q = turn(q, me)
        q = q.reshape(2, T, HH, HD)
        kv_mate = swap_core(kv)[::-1]
        k = jnp.where(c == 0, kv, kv_mate)
        v = jnp.where(c == 0, kv_mate, kv)
        order.mark(kv)
        if aligned:
            out_gather.pass_on()
        q, k = order(q, k)
        s = jnp.einsum("rthd,rjd->rhtj", q, k, preferred_element_type=F32) * HD**-0.5
        s = jnp.where(allowed[:, None], s, -1e30)
        p = jnp.exp(s - jnp.max(s, axis=-1, keepdims=True))
        p = p / jnp.sum(p, axis=-1, keepdims=True)
        if aligned:
            p, pieces, cot_z, down_gather.pieces = lax.optimization_barrier(
                (p, out_gather.pieces, cot_z, down_gather.pieces)
            )
            w_out = jnp.concatenate(pieces)
        pb = p.astype(BF)
        o = jnp.einsum("rhtj,rjd->rthd", pb, v, preferred_element_type=F32)
        o = o.astype(BF).reshape(2 * T, DH)
        order.mark(w_out, cot_z)
        o_w = order(o)
        away = swap_core(mm(o_w[T:], w_out))
        mid = x + bo + mm(o_w[:T], w_out) + away

        xhat2, rstd2 = ln_stats(mid)
        h2 = turn((xhat2 * g2 + b2).astype(BF), me)
        h2_z = gather(h2, "ctx").reshape(Z * T, D)

        order.mark(h2)
        up_gather = ChipGather(order(w_up.reshape(C * Z * R, F)), square)
        half = Z * T
        cot_z, down_pieces = order(cot_z, down_gather.pieces)
        cots = [cot_z, swap_core(cot_z)]
        if square:
            w_down = jnp.zeros((F, D), BF)
            places = [(0, 0), (1, 0), (2, 0), (3, 0), (3, 1)]
            for part, (block, j) in zip(down_pieces, places):
                at = (me ^ block) * F0 + j * (F0 // 2)
                w_down = lax.dynamic_update_slice_in_dim(w_down, part, at, 0)
        else:
            w_down = jnp.concatenate(down_pieces)
        order.mark(w_down)
        up_gather.pass_on()
        dacts = [side(part, w_down, 1, 1) for part in cots]
        w_up = jnp.concatenate(after(up_gather.pieces, dacts))
        order.mark(dacts, w_up)
        h2_z = order(h2_z)
        h2s = [h2_z, swap_core(h2_z)]
        acts, dpres = [], []
        for part, dact in zip(h2s, dacts):
            act, dpre = hidden(part, w_up, bu, dact)
            acts.append(act)
            dpres.append(dpre)
        away = swap_core(side(dpres[1], w_up, 1, 1, BF))
        dh2_part, away = lax.optimization_barrier((side(dpres[0], w_up, 1, 1), away))
        dh2_part = (dh2_part + away.astype(F32)).astype(BF).reshape(Z, T, D)
        order.mark(dh2_part)
        dh2 = turn(scatter(dh2_part, "ctx").astype(F32), me)
        dpre_w, act_w, h2_all, cot_all = (jnp.concatenate(order(*pair)) for pair in (dpres, acts, h2s, cots))

        def down_term(*parts):
            half = F0 // 2
            cols = [
                lax.dynamic_slice_in_dim(act_w, (me ^ i if square else i) * F0 + j * half, half, axis=1)
                for i, j in parts
            ]
            return mm_tn(jnp.concatenate(cols, axis=1), cot_all)

        down_sum = ChipSum(down_term, square, AB)
        order.mark(down_sum.sent)
        up_sum = ChipSum(product(order(h2_all), dpre_w), square, AB)
        out_away = swap_core(mm(order(acts[1]), w_down).astype(BF))
        order.mark(up_sum.sent, out_away)
        down_sum.pass_on(order)
        order.mark(down_sum.sent)
        dh2 = order(dh2)
        order.mark(dh2)
        dmid = cotangent[0].astype(F32) + ln_back(dh2, g2, xhat2, rstd2)
        db = dmid.astype(BF)
        db = jnp.concatenate([db, swap_core(db)])
        do = mm_nt(db, w_out).astype(BF)
        order.mark(do)
        do_h = order(do).reshape(2, T, HH, HD)
        dp = jnp.einsum("rthd,rjd->rhtj", do_h, v, preferred_element_type=F32)
        ds = (p * (dp - jnp.sum(p * dp, axis=-1, keepdims=True))).astype(BF)
        order.mark(ds, down_sum.far)
        ds = order(ds)
        dk = jnp.einsum("rhtj,rthd->rjd", ds, q, preferred_element_type=F32) * HD**-0.5
        dv = jnp.einsum("rhtj,rthd->rjd", pb, do_h, preferred_element_type=F32)
        dkv_away = swap_core(jnp.where(c == 0, dv, dk).astype(BF))
        dkv = jnp.where(c == 0, dk, dv) + dkv_away[::-1].astype(F32)
        dkv = dkv.astype(BF).reshape(2, Z, T, HD).transpose(1, 0, 2, 3)
        order.mark(dkv)
        dkv = lax.all_to_all(dkv, "ctx", 0, 0, tiled=True)
        mlp, out_away = lax.optimization_barrier((side(order(acts[0]), w_down, 1, 0), out_away))
        mlp = (mlp + out_away.astype(F32)).astype(BF).reshape(Z, T, D)
        order.mark(mlp)
        mlp = scatter(mlp, "ctx")
        ds_w = order(ds)
        dq = jnp.einsum("rhtj,rjd->rthd", ds_w, k, preferred_element_type=F32) * HD**-0.5
        dq = dq.astype(BF).reshape(2 * T, DH)
        if aligned:
            dq = turn(dq, me)
        order.mark(dq)
        dkv = order(dkv)
        dkv = jnp.sum(dkv.astype(F32), axis=0).astype(BF).reshape(2 * T, HD)
        dq_ext = jnp.concatenate([dq, dkv], axis=1)
        ext_sum = ChipSum(product(h1, dq_ext), square, AB)
        order.mark(ext_sum.sent)

        dq_w = order(dq_ext)
        dh1_away = swap_core(side(dq_w[T:], w_ext, 1, 1))
        dh1 = turn(side(dq_w[:T], w_ext, 1, 1) + dh1_away, me)
        up_sum.pass_on(order)
        order.mark(up_sum.sent, dh1)
        ext_sum.pass_on(order)
        order.mark(ext_sum.sent)
        if aligned:
            out_sum = ChipSum(product(o, order(db), side), square, AB, ext_sum.far)
            order.mark(out_sum.sent)
        g_ext = ext_sum.finish(order).astype(BF).reshape(2, Z, R, E)
        g_ext = g_ext.transpose(1, 0, 2, 3).reshape(Z, 2 * R, E)
        g_ext, mlp = lax.optimization_barrier((g_ext, mlp))
        order.mark(g_ext)
        g_ext = scatter(g_ext, "ctx").reshape(2, R, E)
        g_up = up_sum.finish(order).astype(BF).reshape(C * Z, R, F)
        order.mark(g_up)
        g_up = lax.all_to_all(g_up, ("core", "ctx"), 0, 0, tiled=True)
        if aligned:
            out_sum.pass_on(order)
            order.mark(out_sum.sent)
            g_out = out_sum.finish(order).astype(BF).reshape(Z, R, D)
            order.mark(g_out)
            g_out = scatter(g_out, "ctx").astype(F32)
        else:
            g_out = mm_tn(o, order(db)).astype(BF)
            full = jnp.where(lax.broadcasted_iota(jnp.int32, (2, 1, 1), 0) == c, g_out[None], 0)
            g_out = scatter(full.reshape(N, R, D), EVERY).astype(F32)
        g_ext, g_up = order(g_ext, g_up)
        order.mark(g_ext, g_up)
        own_core = (lax.broadcasted_iota(jnp.int32, (1, 2, 1), 1) == c).astype(F32)
        own_cz = (lax.broadcasted_iota(jnp.int32, (1, C * Z, 1), 1) == c * Z + z).astype(F32)
        dh2_late, dpre_late, cot_late, dq_late, db_late = order(dh2, dpre_w, cotangent[0], dq_ext, db[:T])
        gb_up = jnp.sum(dpre_late.astype(F32), axis=0)
        gb_ext = jnp.sum(dq_late.astype(F32), axis=0)
        wide = [
            jnp.sum(dh1 * xhat1, axis=0),
            jnp.sum(dh1, axis=0),
            (gb_ext[:DH].reshape(G, 1, W0) * own_core).reshape(D),
            jnp.sum(db_late.astype(F32), axis=0),
            jnp.sum(dh2_late * xhat2, axis=0),
            jnp.sum(dh2_late, axis=0),
            jnp.sum(cot_late.astype(F32), axis=0),
        ]
        packed = jnp.concatenate(
            [w.reshape(N, R) for w in wide]
            + [
                (gb_up.reshape(AB, 1, F0) * own_cz).reshape(N, F0),
                jnp.where(c == 1, gb_ext[DH:], 0.0).reshape(N, vb0),
            ],
            axis=1,
        )
        packed = jnp.sum(lax.all_to_all(packed, EVERY, 0, 0, tiled=True), axis=0)
        g_down = down_sum.finish(order)
        dx = dmid + ln_back(order(dh1), g1, xhat1, rstd1)
        first, second = g_ext[0], g_ext[1]
        mate = swap_core(jnp.where(c == 0, second, first))
        mine = jnp.where(c == 0, first, second)
        first, second = jnp.where(c == 0, mine, mate), jnp.where(c == 0, mate, mine)
        g_q = [h[:, g * W0 : (g + 1) * W0] for g in range(G) for h in (first, second)]
        g_q = jnp.concatenate(g_q, axis=1).astype(F32)
        g_kv = jnp.concatenate([first[:, DH:], second[:, DH:]], axis=1).astype(F32)
        g_up = g_up.reshape(C * Z, R, AB, F0).transpose(1, 2, 0, 3).reshape(R, FF).astype(F32)
        result = order(mid) + mlp.astype(F32) + bd

        vecs = [packed[i * R : (i + 1) * R] for i in range(7)]
        gb_up = packed[7 * R : 7 * R + F0]
        gb_v = packed[7 * R + F0 :]
        return (
            result.astype(BF)[None], dx.astype(BF)[None],
            vecs[0], vecs[1], g_q, vecs[2], g_kv, gb_v, g_out, vecs[3],
            vecs[4], vecs[5], g_up, gb_up, g_down, vecs[6],
        )

    return local


def solution(mesh):
    dp, ctx = mesh.shape["dp"], mesh.shape["ctx"]
    chips = dp // 2
    a = next(i for i in range(int(chips**0.5), 0, -1) if chips % i == 0)
    b = chips // a
    fine = Mesh(mesh.devices.reshape(a, b, 2, ctx), EVERY)
    tok = P(("a", "b", "core"), "ctx", None)
    vec = P(EVERY)
    mat = P(EVERY, None)
    in_specs = (
        tok, P(("a", "b", "core"), None),
        vec, vec, mat, vec, mat, vec, mat, vec, vec, vec, mat, vec, mat, vec, tok,
    )
    out_specs = (tok, tok, vec, vec, mat, vec, mat, vec, mat, vec, vec, vec, mat, vec, mat, vec)
    return jax.shard_map(
        make_local(a, b, ctx), mesh=fine, in_specs=in_specs, out_specs=out_specs, check_vma=False
    )
```

```python
import jax
import jax.numpy as jnp
from jax import lax
from jax.experimental import pallas as pl
from jax.experimental.pallas import tpu as pltpu
from jax.sharding import Mesh, PartitionSpec as P

HEADS = 16
HD = 128
EPS = 1e-05
GELU_K = 0.7978845608028654
GELU_C = 0.044715

BF = jnp.bfloat16
F32 = jnp.float32
CHIP = ("a", "b")
EVERY = ("a", "b", "core", "ctx")
MATES = [(0, 1), (1, 0)]


def dot(a, b, dims):
    return lax.dot_general(a, b, (dims, ((), ())), preferred_element_type=F32)


def mm(a, b):
    return dot(a, b, ((1,), (0,)))


def mm_nt(a, b):
    return dot(a, b, ((1,), (1,)))


def mm_tn(a, b):
    return dot(a, b, ((0,), (0,)))


def side(a, b, ca, cb, out=F32):
    count, cols, depth = a.shape[1 - ca], b.shape[1 - cb], a.shape[ca]
    tile = next((t for t in (512, 384, 256, 128) if cols % t == 0), cols)

    def kernel(a_ref, b_ref, o_ref):
        o_ref[...] = lax.dot_general(
            a_ref[...], b_ref[...], (((ca,), (cb,)), ((), ())), preferred_element_type=F32
        ).astype(out)

    return pl.pallas_call(
        kernel,
        out_shape=jax.ShapeDtypeStruct((count, cols), out),
        grid=(cols // tile,),
        in_specs=[
            pl.BlockSpec(a.shape, lambda j: (0, 0)),
            pl.BlockSpec((depth, tile), lambda j: (0, j)) if cb == 0 else pl.BlockSpec((tile, depth), lambda j: (j, 0)),
        ],
        out_specs=pl.BlockSpec((count, tile), lambda j: (0, j)),
        compiler_params=pltpu.CompilerParams(vmem_limit_bytes=24 << 20),
        cost_estimate=pl.CostEstimate(flops=0, bytes_accessed=0, transcendentals=0),
        name="side",
    )(a, b)


def hidden(h, w_up, bias, dact):
    count, depth = h.shape
    units = w_up.shape[1]
    tile = next((t for t in (256, 128) if units % t == 0), units)

    def kernel(h_ref, w_ref, b_ref, d_ref, act_ref, dpre_ref):
        pre = jnp.dot(h_ref[...], w_ref[...], preferred_element_type=F32) + b_ref[...]
        square = pre * pre
        th = jnp.tanh(GELU_K * pre * (1.0 + GELU_C * square))
        half = 0.5 * (1.0 + th)
        act_ref[...] = (pre * half).astype(BF)
        slope = half + 0.5 * GELU_K * pre * (1.0 - th * th) * (1.0 + 3.0 * GELU_C * square)
        dpre_ref[...] = (d_ref[...] * slope).astype(BF)

    return pl.pallas_call(
        kernel,
        out_shape=[jax.ShapeDtypeStruct((count, units), BF)] * 2,
        grid=(units // tile,),
        in_specs=[
            pl.BlockSpec((count, depth), lambda j: (0, 0)),
            pl.BlockSpec((depth, tile), lambda j: (0, j)),
            pl.BlockSpec((1, tile), lambda j: (0, j)),
            pl.BlockSpec((count, tile), lambda j: (0, j)),
        ],
        out_specs=[pl.BlockSpec((count, tile), lambda j: (0, j))] * 2,
        compiler_params=pltpu.CompilerParams(vmem_limit_bytes=24 << 20),
        cost_estimate=pl.CostEstimate(
            flops=2 * count * depth * units, bytes_accessed=2 * (count + units) * depth, transcendentals=count * units
        ),
        name="hidden",
    )(h, w_up, bias.reshape(1, units), dact)


def ln_stats(x):
    mean = jnp.mean(x, axis=-1, keepdims=True)
    cen = x - mean
    var = jnp.mean(cen * cen, axis=-1, keepdims=True)
    rstd = lax.rsqrt(var + EPS)
    return cen * rstd, rstd


def ln_back(dh, gain, xhat, rstd):
    e = dh * gain
    me = jnp.mean(e, axis=-1, keepdims=True)
    mx = jnp.mean(e * xhat, axis=-1, keepdims=True)
    return (e - me - xhat * mx) * rstd


def after(x, *others):
    return lax.optimization_barrier((x, others))[0]


def swap_core(x):
    return lax.ppermute(x, "core", MATES)


def over_a(x):
    return lax.ppermute(x, "a", MATES)


def over_b(x):
    return lax.ppermute(x, "b", MATES)


def gather(x, axes):
    return lax.all_gather(x, axes, axis=0, tiled=False)


def scatter(x, axes):
    return lax.psum_scatter(x, axes, scatter_dimension=0, tiled=False)


class Order:
    def __init__(self):
        self.last = []

    def mark(self, *done):
        self.last = list(done)

    def __call__(self, *xs):
        xs = lax.optimization_barrier((xs, self.last))[0]
        return xs[0] if len(xs) == 1 else xs


class ChipGather:
    def __init__(self, x, square):
        self.square = square
        if not square:
            self.pieces = list(gather(x, CHIP).reshape((-1,) + x.shape))
            return
        self.pieces = [x, over_b(x), over_a(x)]

    def pass_on(self, *joint):
        if self.square:
            x, x1, x2 = self.pieces
            (x1, x2), joint = lax.optimization_barrier(((x1, x2), joint))
            half = x.shape[0] // 2
            self.pieces = [x, x1, x2, over_a(x1[:half]), over_b(x2[half:])]
        return joint


class ChipSum:
    def __init__(self, term, square, count, gate=()):
        self.square, self.term = square, term
        self.far = []
        if not square:
            full = jnp.stack([term((i, 0), (i, 1)) for i in range(count)])
            self.result = scatter(full.astype(BF), CHIP).astype(F32)
            self.sent = [full]
            return
        u = term((3, 0), (1, 0)).astype(BF)
        w = term((3, 1), (2, 1)).astype(BF)
        self.sent = [u, w]
        if gate:
            u, w = after((u, w), *gate)
        self.near = [over_b(u), over_a(w)]

    def pass_on(self, order):
        if self.square:
            u, w = self.near = order(*self.near)
            half = u.shape[0] // 2
            u = (self.term((2, 0)) + u[:half].astype(F32)).astype(BF)
            w = (self.term((1, 1)) + w[:half].astype(F32)).astype(BF)
            self.sent = [u, w]
            self.far = [over_a(u), over_b(w)]

    def finish(self, order, free=False):
        if not self.square:
            return self.result
        f0, f1 = order(*self.far)
        half = f0.shape[0]
        n0, n1 = self.near[0][half:], self.near[1][half:]
        return self.term((0, 0), (0, 1), free=free) + (
            jnp.concatenate([n0, n1]).astype(F32) + jnp.concatenate([f0, f1]).astype(F32)
        )


def make_local(A, B, Z):
    C = 2
    AB = A * B
    N = AB * C * Z
    square = A == 2 and B == 2

    def turn(x, me):
        if not square:
            return x
        w = x.shape[1] // AB
        cols = [x[:, i * w : (i + 1) * w] for i in range(AB)]
        return jnp.concatenate([lax.select_n(me ^ i, *cols) for i in range(AB)], axis=1)

    def product(left, right, multiply=None):
        half = left.shape[1] // AB // 2

        def term(*parts, free=False):
            cols = [left[:, (2 * i + j) * half : (2 * i + j + 1) * half] for i, j in parts]
            cols = jnp.concatenate(cols, axis=1)
            return side(cols, right, 0, 0) if free or multiply is not None else mm_tn(cols, right)

        return term

    def local(
        activations, segment_ids,
        ln1_gain, ln1_bias, q_weight, q_bias, kv_weight, v_bias, out_weight, out_bias,
        ln2_gain, ln2_bias, up_weight, up_bias, down_weight, down_bias, cotangent,
    ):
        T, D = activations.shape[1:]
        S = segment_ids.shape[1]
        R = q_weight.shape[0]
        F0 = down_weight.shape[0]
        F = AB * F0
        FF = up_weight.shape[1]
        DH = D // 2
        HH = HEADS // 2
        aligned = (Z * R) % HD == 0
        G = AB if aligned else 1
        W0 = DH // G
        E = DH + HD
        c = lax.axis_index("core")
        z = lax.axis_index("ctx")
        me = lax.axis_index("a") * B + lax.axis_index("b")

        order = Order()

        def half_of(i):
            cols = [q_weight[:, (g * 2 + i) * W0 : (g * 2 + i + 1) * W0] for g in range(G)]
            return jnp.concatenate(cols + [kv_weight[:, i * HD : (i + 1) * HD]], axis=1)

        first, second = half_of(0), half_of(1)
        mine = jnp.where(c == 0, first, second)
        mate = swap_core(jnp.where(c == 0, second, first))
        w_ext = jnp.concatenate([jnp.where(c == 0, mine, mate), jnp.where(c == 0, mate, mine)])
        order.mark(w_ext)
        w_ext_z = gather(w_ext, "ctx").reshape(Z, 2, R, E).transpose(1, 0, 2, 3).reshape(2 * Z * R, E)

        down_gather = ChipGather(order(down_weight), square)
        order.mark(w_ext)
        small, xin = order(
            [ln1_gain, ln1_bias, q_bias, out_bias, ln2_gain, ln2_bias, down_bias, up_bias, v_bias], activations[0]
        )
        vb0 = v_bias.shape[0]
        small = jnp.concatenate(small)
        small = jnp.broadcast_to(small[None], (N, small.shape[0]))
        small = lax.all_to_all(small, EVERY, 0, 0, tiled=True).astype(F32)
        g1, b1, bq, bo, g2, b2, bd = (small[:, i * R : (i + 1) * R].reshape(D) for i in range(7))
        bu = small[:, 7 * R : 7 * R + F0].reshape(AB, C * Z, F0)
        bu = lax.dynamic_index_in_dim(bu, c * Z + z, 1, keepdims=False).reshape(F)
        bv = small[:, 7 * R + F0 :].reshape(HD)
        bq = lax.dynamic_index_in_dim(bq.reshape(G, 2, W0), c, 1, keepdims=False).reshape(DH)
        b_ext = jnp.concatenate([bq, jnp.where(c == 1, bv, 0.0)])
        x = xin.astype(F32)
        xhat1, rstd1 = ln_stats(x)
        h1 = turn((xhat1 * g1 + b1).astype(BF), me)
        h1 = jnp.concatenate([h1, swap_core(h1)])
        seg = jnp.concatenate([segment_ids, swap_core(segment_ids)])
        start = z * T
        seg_q = lax.dynamic_slice_in_dim(seg, start, T, axis=1)
        q_at = start + jnp.arange(T, dtype=jnp.int32)
        k_at = jnp.arange(S, dtype=jnp.int32)
        allowed = (k_at[None, None, :] <= q_at[None, :, None]) & (seg[:, None, :] == seg_q[:, :, None])
        out_in = after(out_weight, w_ext_z)
        up_in = after(up_weight, w_ext_z)
        w_ext_z = order(w_ext_z)
        ext_gather = ChipGather(w_ext_z, square)
        if aligned:
            w_out_z = gather(out_in, "ctx").reshape(Z * R, D)
        else:
            w_out = gather(out_in, EVERY).reshape(2, DH, D)
            w_out = w_out_z = lax.dynamic_index_in_dim(w_out, c, 0, keepdims=False)
        up_cols = [
            jnp.concatenate([up_in[:, (i * C * Z + j) * F0 : (i * C * Z + j + 1) * F0] for i in range(AB)], axis=1)
            for j in range(C * Z)
        ]
        w_up = lax.all_to_all(jnp.stack(up_cols), ("core", "ctx"), 0, 0, tiled=True)
        w_out_z, down_gather.pieces = ext_gather.pass_on(w_out_z, down_gather.pieces)
        down_gather.pass_on()
        ext_gather.pieces, w_up = lax.optimization_barrier((ext_gather.pieces, w_up))

        w_ext = jnp.concatenate(ext_gather.pieces)
        order.mark(w_ext)
        h1 = order(h1)
        if aligned:
            out_gather = ChipGather(w_out_z, square)
        cot_z = gather(after(cotangent[0], w_out_z), "ctx").reshape(Z * T, D)
        q_ext = (mm(h1, w_ext) + b_ext).astype(BF)
        kv = gather(q_ext[:, DH:].reshape(2, T, HD), "ctx").transpose(1, 0, 2, 3).reshape(2, S, HD)
        q = q_ext[:, :DH]
        if aligned:
            q = turn(q, me)
        q = q.reshape(2, T, HH, HD)
        kv_mate = swap_core(kv)[::-1]
        k = jnp.where(c == 0, kv, kv_mate)
        v = jnp.where(c == 0, kv_mate, kv)
        order.mark(kv)
        if aligned:
            out_gather.pass_on()
        q, k = order(q, k)
        s = jnp.einsum("rthd,rjd->rhtj", q, k, preferred_element_type=F32) * HD**-0.5
        s = jnp.where(allowed[:, None], s, -1e30)
        p = jnp.exp(s - jnp.max(s, axis=-1, keepdims=True))
        p = p / jnp.sum(p, axis=-1, keepdims=True)
        if aligned:
            p, pieces, cot_z, down_gather.pieces = lax.optimization_barrier(
                (p, out_gather.pieces, cot_z, down_gather.pieces)
            )
            w_out = jnp.concatenate(pieces)
        pb = p.astype(BF)
        o = jnp.einsum("rhtj,rjd->rthd", pb, v, preferred_element_type=F32)
        o = o.astype(BF).reshape(2 * T, DH)
        order.mark(w_out, cot_z)
        o_w = order(o)
        away = swap_core(mm(o_w[T:], w_out))
        mid = x + bo + mm(o_w[:T], w_out) + away

        xhat2, rstd2 = ln_stats(mid)
        h2 = turn((xhat2 * g2 + b2).astype(BF), me)
        h2_z = gather(h2, "ctx").reshape(Z * T, D)

        order.mark(h2)
        up_gather = ChipGather(order(w_up.reshape(C * Z * R, F)), square)
        half = Z * T
        cot_z, down_pieces = order(cot_z, down_gather.pieces)
        cots = [cot_z, swap_core(cot_z)]
        if square:
            w_down = jnp.zeros((F, D), BF)
            places = [(0, 0), (1, 0), (2, 0), (3, 0), (3, 1)]
            for part, (block, j) in zip(down_pieces, places):
                at = (me ^ block) * F0 + j * (F0 // 2)
                w_down = lax.dynamic_update_slice_in_dim(w_down, part, at, 0)
        else:
            w_down = jnp.concatenate(down_pieces)
        order.mark(w_down)
        up_gather.pass_on()
        dacts = [side(part, w_down, 1, 1) for part in cots]
        w_up = jnp.concatenate(after(up_gather.pieces, dacts))
        order.mark(dacts, w_up)
        h2_z = order(h2_z)
        h2s = [h2_z, swap_core(h2_z)]
        acts, dpres = [], []
        for part, dact in zip(h2s, dacts):
            act, dpre = hidden(part, w_up, bu, dact)
            acts.append(act)
            dpres.append(dpre)
        away = swap_core(side(dpres[1], w_up, 1, 1, BF))
        dh2_part, away = lax.optimization_barrier((side(dpres[0], w_up, 1, 1), away))
        dh2_part = (dh2_part + away.astype(F32)).astype(BF).reshape(Z, T, D)
        order.mark(dh2_part)
        dh2 = turn(scatter(dh2_part, "ctx").astype(F32), me)
        dpre_w, act_w, h2_all, cot_all = (jnp.concatenate(order(*pair)) for pair in (dpres, acts, h2s, cots))

        def down_term(*parts, free=False):
            half = F0 // 2
            cols = [
                lax.dynamic_slice_in_dim(act_w, (me ^ i if square else i) * F0 + j * half, half, axis=1)
                for i, j in parts
            ]
            cols = jnp.concatenate(cols, axis=1)
            return side(cols, cot_all, 0, 0) if free else mm_tn(cols, cot_all)

        down_sum = ChipSum(down_term, square, AB)
        order.mark(down_sum.sent)
        up_sum = ChipSum(product(order(h2_all), dpre_w), square, AB)
        out_away = swap_core(mm(order(acts[1]), w_down).astype(BF))
        order.mark(up_sum.sent, out_away)
        down_sum.pass_on(order)
        order.mark(down_sum.sent)
        dh2 = order(dh2)
        order.mark(dh2)
        dmid = cotangent[0].astype(F32) + ln_back(dh2, g2, xhat2, rstd2)
        db = dmid.astype(BF)
        db = jnp.concatenate([db, swap_core(db)])
        do = mm_nt(db, w_out).astype(BF)
        order.mark(do)
        do_h = order(do).reshape(2, T, HH, HD)
        dp = jnp.einsum("rthd,rjd->rhtj", do_h, v, preferred_element_type=F32)
        ds = (p * (dp - jnp.sum(p * dp, axis=-1, keepdims=True))).astype(BF)
        order.mark(ds, down_sum.far)
        ds = order(ds)
        dk = jnp.einsum("rhtj,rthd->rjd", ds, q, preferred_element_type=F32) * HD**-0.5
        dv = jnp.einsum("rhtj,rthd->rjd", pb, do_h, preferred_element_type=F32)
        dkv_away = swap_core(jnp.where(c == 0, dv, dk).astype(BF))
        dkv = jnp.where(c == 0, dk, dv) + dkv_away[::-1].astype(F32)
        dkv = dkv.astype(BF).reshape(2, Z, T, HD).transpose(1, 0, 2, 3)
        order.mark(dkv)
        dkv = lax.all_to_all(dkv, "ctx", 0, 0, tiled=True)
        mlp, out_away = lax.optimization_barrier((side(order(acts[0]), w_down, 1, 0), out_away))
        mlp = (mlp + out_away.astype(F32)).astype(BF).reshape(Z, T, D)
        order.mark(mlp)
        mlp = scatter(mlp, "ctx")
        ds_w = order(ds)
        dq = jnp.einsum("rhtj,rjd->rthd", ds_w, k, preferred_element_type=F32) * HD**-0.5
        dq = dq.astype(BF).reshape(2 * T, DH)
        if aligned:
            dq = turn(dq, me)
        order.mark(dq)
        dkv = order(dkv)
        dkv = jnp.sum(dkv.astype(F32), axis=0).astype(BF).reshape(2 * T, HD)
        dq_ext = jnp.concatenate([dq, dkv], axis=1)
        ext_sum = ChipSum(product(h1, dq_ext), square, AB)
        order.mark(ext_sum.sent)

        dq_w = order(dq_ext)
        dh1_away = swap_core(side(dq_w[T:], w_ext, 1, 1))
        dh1 = turn(side(dq_w[:T], w_ext, 1, 1) + dh1_away, me)
        up_sum.pass_on(order)
        order.mark(up_sum.sent, dh1)
        ext_sum.pass_on(order)
        order.mark(ext_sum.sent)
        if aligned:
            out_sum = ChipSum(product(o, order(db), side), square, AB, ext_sum.far)
            order.mark(out_sum.sent)
        dx = (dmid + ln_back(dh1, g1, xhat1, rstd1)).astype(BF)
        result = (mid + mlp.astype(F32) + bd).astype(BF)
        ext_sum.far, dx, result = lax.optimization_barrier((ext_sum.far, dx, result))
        g_ext = ext_sum.finish(order).astype(BF).reshape(2, Z, R, E)
        g_ext = g_ext.transpose(1, 0, 2, 3).reshape(Z, 2 * R, E)
        order.mark(g_ext)
        g_ext = scatter(g_ext, "ctx").reshape(2, R, E)
        g_up = up_sum.finish(order).astype(BF).reshape(C * Z, R, F)
        order.mark(g_up)
        g_up = lax.all_to_all(g_up, ("core", "ctx"), 0, 0, tiled=True)
        first, second = g_ext[0], g_ext[1]
        mate = swap_core(jnp.where(c == 0, second, first))
        mine = jnp.where(c == 0, first, second)
        first, second = jnp.where(c == 0, mine, mate), jnp.where(c == 0, mate, mine)
        g_q = [h[:, g * W0 : (g + 1) * W0] for g in range(G) for h in (first, second)]
        g_q = jnp.concatenate(g_q, axis=1).astype(F32)
        g_kv = jnp.concatenate([first[:, DH:], second[:, DH:]], axis=1).astype(F32)
        g_down = down_sum.finish(order, free=True)
        if aligned:
            if square:
                out_sum.near, g_down = lax.optimization_barrier((out_sum.near, g_down))
            out_sum.pass_on(order)
            order.mark(out_sum.sent)
            if square:
                out_sum.far, g_q, g_kv = lax.optimization_barrier((out_sum.far, g_q, g_kv))
            g_out = out_sum.finish(order).astype(BF).reshape(Z, R, D)
            order.mark(g_out)
            g_out = scatter(g_out, "ctx").astype(F32)
        else:
            g_out = mm_tn(o, order(db)).astype(BF)
            full = jnp.where(lax.broadcasted_iota(jnp.int32, (2, 1, 1), 0) == c, g_out[None], 0)
            g_out = scatter(full.reshape(N, R, D), EVERY).astype(F32)
        own_core = (lax.broadcasted_iota(jnp.int32, (1, 2, 1), 1) == c).astype(F32)
        own_cz = (lax.broadcasted_iota(jnp.int32, (1, C * Z, 1), 1) == c * Z + z).astype(F32)
        dh2_late, dpre_late, cot_late, dq_late, db_late = order(dh2, dpre_w, cotangent[0], dq_ext, db[:T])
        gb_up = jnp.sum(dpre_late.astype(F32), axis=0)
        gb_ext = jnp.sum(dq_late.astype(F32), axis=0)
        wide = [
            jnp.sum(dh1 * xhat1, axis=0),
            jnp.sum(dh1, axis=0),
            (gb_ext[:DH].reshape(G, 1, W0) * own_core).reshape(D),
            jnp.sum(db_late.astype(F32), axis=0),
            jnp.sum(dh2_late * xhat2, axis=0),
            jnp.sum(dh2_late, axis=0),
            jnp.sum(cot_late.astype(F32), axis=0),
        ]
        packed = jnp.concatenate(
            [w.reshape(N, R) for w in wide]
            + [
                (gb_up.reshape(AB, 1, F0) * own_cz).reshape(N, F0),
                jnp.where(c == 1, gb_ext[DH:], 0.0).reshape(N, vb0),
            ],
            axis=1,
        )
        packed = jnp.sum(lax.all_to_all(packed, EVERY, 0, 0, tiled=True), axis=0)
        g_up = g_up.reshape(C * Z, R, AB, F0).transpose(1, 2, 0, 3).reshape(R, FF).astype(F32)

        vecs = [packed[i * R : (i + 1) * R] for i in range(7)]
        gb_up = packed[7 * R : 7 * R + F0]
        gb_v = packed[7 * R + F0 :]
        return (
            result[None], dx[None],
            vecs[0], vecs[1], g_q, vecs[2], g_kv, gb_v, g_out, vecs[3],
            vecs[4], vecs[5], g_up, gb_up, g_down, vecs[6],
        )

    return local


def solution(mesh):
    dp, ctx = mesh.shape["dp"], mesh.shape["ctx"]
    chips = dp // 2
    a = next(i for i in range(int(chips**0.5), 0, -1) if chips % i == 0)
    b = chips // a
    fine = Mesh(mesh.devices.reshape(a, b, 2, ctx), EVERY)
    tok = P(("a", "b", "core"), "ctx", None)
    vec = P(EVERY)
    mat = P(EVERY, None)
    in_specs = (
        tok, P(("a", "b", "core"), None),
        vec, vec, mat, vec, mat, vec, mat, vec, vec, vec, mat, vec, mat, vec, tok,
    )
    out_specs = (tok, tok, vec, vec, mat, vec, mat, vec, mat, vec, vec, vec, mat, vec, mat, vec)
    return jax.shard_map(
        make_local(a, b, ctx), mesh=fine, in_specs=in_specs, out_specs=out_specs, check_vma=False
    )
```

```python
import jax
import jax.numpy as jnp
from jax import lax
from jax.experimental import pallas as pl
from jax.experimental.pallas import tpu as pltpu
from jax.sharding import Mesh, PartitionSpec as P

HEADS = 16
HD = 128
EPS = 1e-05
GELU_K = 0.7978845608028654
GELU_C = 0.044715

BF = jnp.bfloat16
F32 = jnp.float32
CHIP = ("a", "b")
EVERY = ("a", "b", "core", "ctx")
MATES = [(0, 1), (1, 0)]


def dot(a, b, dims):
    return lax.dot_general(a, b, (dims, ((), ())), preferred_element_type=F32)


def mm(a, b):
    return dot(a, b, ((1,), (0,)))


def mm_nt(a, b):
    return dot(a, b, ((1,), (1,)))


def mm_tn(a, b):
    return dot(a, b, ((0,), (0,)))


def side(a, b, ca, cb, out=F32):
    count, cols, depth = a.shape[1 - ca], b.shape[1 - cb], a.shape[ca]
    tile = next((t for t in (512, 384, 256, 128) if cols % t == 0), cols)

    def kernel(a_ref, b_ref, o_ref):
        o_ref[...] = lax.dot_general(
            a_ref[...], b_ref[...], (((ca,), (cb,)), ((), ())), preferred_element_type=F32
        ).astype(out)

    return pl.pallas_call(
        kernel,
        out_shape=jax.ShapeDtypeStruct((count, cols), out),
        grid=(cols // tile,),
        in_specs=[
            pl.BlockSpec(a.shape, lambda j: (0, 0)),
            pl.BlockSpec((depth, tile), lambda j: (0, j)) if cb == 0 else pl.BlockSpec((tile, depth), lambda j: (j, 0)),
        ],
        out_specs=pl.BlockSpec((count, tile), lambda j: (0, j)),
        compiler_params=pltpu.CompilerParams(vmem_limit_bytes=24 << 20),
        cost_estimate=pl.CostEstimate(flops=0, bytes_accessed=0, transcendentals=0),
        name="side",
    )(a, b)


def tile_of(cols, largest):
    return next((t for t in (512, 384, 256, 128) if t <= largest and cols % t == 0), cols)


def against(x, refs):
    total, at = None, 0
    for ref in refs:
        depth = ref.shape[0]
        part = jnp.dot(x[:, at : at + depth], ref[...], preferred_element_type=F32)
        total, at = part if total is None else total + part, at + depth
    return total


def cost(count, depth, cols, special=0):
    return pl.CostEstimate(
        flops=2 * count * depth * cols, bytes_accessed=2 * (count + cols) * depth, transcendentals=special
    )


def mm_pieces(x, pieces, bias=None, out=F32):
    count, depth = x.shape
    cols = pieces[0].shape[1]
    tile = tile_of(cols, 512)
    bias = jnp.zeros((cols,), F32) if bias is None else bias

    def kernel(x_ref, b_ref, *refs):
        refs[-1][...] = (against(x_ref, refs[:-1]) + b_ref[...]).astype(out)

    return pl.pallas_call(
        kernel,
        out_shape=jax.ShapeDtypeStruct((count, cols), out),
        grid=(cols // tile,),
        in_specs=[pl.BlockSpec((count, depth), lambda j: (0, 0)), pl.BlockSpec((1, tile), lambda j: (0, j))]
        + [pl.BlockSpec((p.shape[0], tile), lambda j: (0, j)) for p in pieces],
        out_specs=pl.BlockSpec((count, tile), lambda j: (0, j)),
        compiler_params=pltpu.CompilerParams(vmem_limit_bytes=24 << 20),
        cost_estimate=cost(count, depth, cols),
        name="rows_product",
    )(x, bias.reshape(1, cols), *pieces)


def mm_nt_pieces(x, pieces, out=F32):
    count, depth = x.shape
    cols = sum(p.shape[0] for p in pieces)

    def kernel(x_ref, *refs):
        at = 0
        for ref in refs[:-1]:
            part = lax.dot_general(x_ref[...], ref[...], (((1,), (1,)), ((), ())), preferred_element_type=F32)
            refs[-1][:, at : at + ref.shape[0]] = part.astype(out)
            at += ref.shape[0]

    return pl.pallas_call(
        kernel,
        out_shape=jax.ShapeDtypeStruct((count, cols), out),
        compiler_params=pltpu.CompilerParams(vmem_limit_bytes=32 << 20),
        cost_estimate=cost(count, depth, cols),
        name="columns_product",
    )(x, *pieces)


def hidden(h, w_up, bias, dact):
    count, depth = h.shape
    units = w_up.shape[1]
    tile = tile_of(units, 256)

    def kernel(h_ref, w_ref, b_ref, d_ref, act_ref, dpre_ref):
        @pl.loop(0, units // tile)
        def _(step):
            at = pl.ds(pl.multiple_of(step * tile, tile), tile)
            pre = jnp.dot(h_ref[...], w_ref[:, at], preferred_element_type=F32) + b_ref[:, at]
            square = pre * pre
            th = jnp.tanh(GELU_K * pre * (1.0 + GELU_C * square))
            half = 0.5 * (1.0 + th)
            act_ref[:, at] = (pre * half).astype(BF)
            slope = half + 0.5 * GELU_K * pre * (1.0 - th * th) * (1.0 + 3.0 * GELU_C * square)
            dpre_ref[:, at] = (d_ref[:, at] * slope).astype(BF)

    near = pl.BlockSpec(memory_space=pltpu.VMEM)
    return pl.pallas_call(
        kernel,
        out_shape=[jax.ShapeDtypeStruct((count, units), BF)] * 2,
        in_specs=[near] * 4,
        out_specs=[near] * 2,
        compiler_params=pltpu.CompilerParams(vmem_limit_bytes=16 << 20),
        cost_estimate=cost(count, depth, units, count * units),
        name="hidden",
    )(h, w_up, bias.reshape(1, units), dact)


def near_nt(x, w, out):
    count, depth = x.shape
    cols = w.shape[0]
    tile = tile_of(cols, 512)

    def kernel(x_ref, w_ref, o_ref):
        @pl.loop(0, cols // tile)
        def _(step):
            at = pl.ds(pl.multiple_of(step * tile, tile), tile)
            o_ref[:, at] = lax.dot_general(
                x_ref[...], w_ref[at, :], (((1,), (1,)), ((), ())), preferred_element_type=F32
            ).astype(out)

    near = pl.BlockSpec(memory_space=pltpu.VMEM)
    return pl.pallas_call(
        kernel,
        out_shape=jax.ShapeDtypeStruct((count, cols), out),
        in_specs=[near] * 2,
        out_specs=near,
        compiler_params=pltpu.CompilerParams(vmem_limit_bytes=16 << 20),
        cost_estimate=cost(count, depth, cols),
        name="near_product",
    )(x, w)


def ln_stats(x):
    mean = jnp.mean(x, axis=-1, keepdims=True)
    cen = x - mean
    var = jnp.mean(cen * cen, axis=-1, keepdims=True)
    rstd = lax.rsqrt(var + EPS)
    return cen * rstd, rstd


def ln_back(dh, gain, xhat, rstd):
    e = dh * gain
    me = jnp.mean(e, axis=-1, keepdims=True)
    mx = jnp.mean(e * xhat, axis=-1, keepdims=True)
    return (e - me - xhat * mx) * rstd


def after(x, *others):
    return lax.optimization_barrier((x, others))[0]


def swap_core(x):
    return lax.ppermute(x, "core", MATES)


def over_a(x):
    return lax.ppermute(x, "a", MATES)


def over_b(x):
    return lax.ppermute(x, "b", MATES)


def gather(x, axes):
    return lax.all_gather(x, axes, axis=0, tiled=False)


def scatter(x, axes):
    return lax.psum_scatter(x, axes, scatter_dimension=0, tiled=False)


class Order:
    def __init__(self):
        self.last = []

    def mark(self, *done):
        self.last = list(done)

    def __call__(self, *xs):
        xs = lax.optimization_barrier((xs, self.last))[0]
        return xs[0] if len(xs) == 1 else xs


class ChipGather:
    def __init__(self, x, square):
        self.square = square
        if not square:
            self.pieces = list(gather(x, CHIP).reshape((-1,) + x.shape))
            return
        self.pieces = [x, over_b(x), over_a(x)]

    def pass_on(self, *joint):
        if self.square:
            x, x1, x2 = self.pieces
            (x1, x2), joint = lax.optimization_barrier(((x1, x2), joint))
            half = x.shape[0] // 2
            self.pieces = [x, x1, x2, over_a(x1[:half]), over_b(x2[half:])]
        return joint


class ChipSum:
    def __init__(self, term, square, count, gate=()):
        self.square, self.term = square, term
        self.far = []
        if not square:
            full = jnp.stack([term((i, 0), (i, 1)) for i in range(count)])
            self.result = scatter(full.astype(BF), CHIP).astype(F32)
            self.sent = [full]
            return
        u = term((3, 0), (1, 0)).astype(BF)
        w = term((3, 1), (2, 1)).astype(BF)
        self.sent = [u, w]
        if gate:
            u, w = after((u, w), *gate)
        self.near = [over_b(u), over_a(w)]

    def pass_on(self, order):
        if self.square:
            u, w = self.near = order(*self.near)
            half = u.shape[0] // 2
            u = (self.term((2, 0)) + u[:half].astype(F32)).astype(BF)
            w = (self.term((1, 1)) + w[:half].astype(F32)).astype(BF)
            self.sent = [u, w]
            self.far = [over_a(u), over_b(w)]

    def finish(self, order, free=False):
        if not self.square:
            return self.result
        f0, f1 = order(*self.far)
        half = f0.shape[0]
        n0, n1 = self.near[0][half:], self.near[1][half:]
        return self.term((0, 0), (0, 1), free=free) + (
            jnp.concatenate([n0, n1]).astype(F32) + jnp.concatenate([f0, f1]).astype(F32)
        )


def make_local(A, B, Z):
    C = 2
    AB = A * B
    N = AB * C * Z
    square = A == 2 and B == 2

    def turn(x, me):
        if not square:
            return x
        w = x.shape[1] // AB
        cols = [x[:, i * w : (i + 1) * w] for i in range(AB)]
        return jnp.concatenate([lax.select_n(me ^ i, *cols) for i in range(AB)], axis=1)

    def product(left, right, multiply=None):
        half = left.shape[1] // AB // 2

        def term(*parts, free=False):
            cols = [left[:, (2 * i + j) * half : (2 * i + j + 1) * half] for i, j in parts]
            cols = jnp.concatenate(cols, axis=1)
            return side(cols, right, 0, 0) if free or multiply is not None else mm_tn(cols, right)

        return term

    def local(
        activations, segment_ids,
        ln1_gain, ln1_bias, q_weight, q_bias, kv_weight, v_bias, out_weight, out_bias,
        ln2_gain, ln2_bias, up_weight, up_bias, down_weight, down_bias, cotangent,
    ):
        T, D = activations.shape[1:]
        S = segment_ids.shape[1]
        R = q_weight.shape[0]
        F0 = down_weight.shape[0]
        F = AB * F0
        FF = up_weight.shape[1]
        DH = D // 2
        HH = HEADS // 2
        aligned = (Z * R) % HD == 0
        G = AB if aligned else 1
        W0 = DH // G
        E = DH + HD
        c = lax.axis_index("core")
        z = lax.axis_index("ctx")
        me = lax.axis_index("a") * B + lax.axis_index("b")

        order = Order()

        def half_of(i):
            cols = [q_weight[:, (g * 2 + i) * W0 : (g * 2 + i + 1) * W0] for g in range(G)]
            return jnp.concatenate(cols + [kv_weight[:, i * HD : (i + 1) * HD]], axis=1)

        first, second = half_of(0), half_of(1)
        mine = jnp.where(c == 0, first, second)
        mate = swap_core(jnp.where(c == 0, second, first))
        w_ext = jnp.concatenate([jnp.where(c == 0, mine, mate), jnp.where(c == 0, mate, mine)])
        order.mark(w_ext)
        w_ext_z = gather(w_ext, "ctx").reshape(Z, 2, R, E).transpose(1, 0, 2, 3).reshape(2 * Z * R, E)

        down_gather = ChipGather(order(down_weight), square)
        order.mark(w_ext)
        small, xin = order(
            [ln1_gain, ln1_bias, q_bias, out_bias, ln2_gain, ln2_bias, down_bias, up_bias, v_bias], activations[0]
        )
        vb0 = v_bias.shape[0]
        small = jnp.concatenate(small)
        small = jnp.broadcast_to(small[None], (N, small.shape[0]))
        small = lax.all_to_all(small, EVERY, 0, 0, tiled=True).astype(F32)
        g1, b1, bq, bo, g2, b2, bd = (small[:, i * R : (i + 1) * R].reshape(D) for i in range(7))
        bu = small[:, 7 * R : 7 * R + F0].reshape(AB, C * Z, F0)
        bu = lax.dynamic_index_in_dim(bu, c * Z + z, 1, keepdims=False).reshape(F)
        bv = small[:, 7 * R + F0 :].reshape(HD)
        bq = lax.dynamic_index_in_dim(bq.reshape(G, 2, W0), c, 1, keepdims=False).reshape(DH)
        b_ext = jnp.concatenate([bq, jnp.where(c == 1, bv, 0.0)])
        x = xin.astype(F32)
        xhat1, rstd1 = ln_stats(x)
        h1 = turn((xhat1 * g1 + b1).astype(BF), me)
        h1 = jnp.concatenate([h1, swap_core(h1)])
        seg = jnp.concatenate([segment_ids, swap_core(segment_ids)])
        start = z * T
        seg_q = lax.dynamic_slice_in_dim(seg, start, T, axis=1)
        q_at = start + jnp.arange(T, dtype=jnp.int32)
        k_at = jnp.arange(S, dtype=jnp.int32)
        allowed = (k_at[None, None, :] <= q_at[None, :, None]) & (seg[:, None, :] == seg_q[:, :, None])
        out_in = after(out_weight, w_ext_z)
        up_in = after(up_weight, w_ext_z)
        w_ext_z = order(w_ext_z)
        ext_gather = ChipGather(w_ext_z, square)
        if aligned:
            w_out_z = gather(out_in, "ctx").reshape(Z * R, D)
        else:
            w_out = gather(out_in, EVERY).reshape(2, DH, D)
            w_out_z = lax.dynamic_index_in_dim(w_out, c, 0, keepdims=False)
            w_out = [w_out_z]
        up_cols = [
            jnp.concatenate([up_in[:, (i * C * Z + j) * F0 : (i * C * Z + j + 1) * F0] for i in range(AB)], axis=1)
            for j in range(C * Z)
        ]
        w_up = lax.all_to_all(jnp.stack(up_cols), ("core", "ctx"), 0, 0, tiled=True)
        w_out_z, down_gather.pieces = ext_gather.pass_on(w_out_z, down_gather.pieces)
        down_gather.pass_on()
        ext_gather.pieces, w_up = lax.optimization_barrier((ext_gather.pieces, w_up))

        w_ext = jnp.concatenate(ext_gather.pieces)
        order.mark(w_ext)
        h1 = order(h1)
        if aligned:
            out_gather = ChipGather(w_out_z, square)
        cot_z = gather(after(cotangent[0], w_out_z), "ctx").reshape(Z * T, D)
        q_ext = (mm(h1, w_ext) + b_ext).astype(BF)
        kv = gather(q_ext[:, DH:].reshape(2, T, HD), "ctx").transpose(1, 0, 2, 3).reshape(2, S, HD)
        q = q_ext[:, :DH]
        if aligned:
            q = turn(q, me)
        q = q.reshape(2, T, HH, HD)
        kv_mate = swap_core(kv)[::-1]
        k = jnp.where(c == 0, kv, kv_mate)
        v = jnp.where(c == 0, kv_mate, kv)
        order.mark(kv)
        if aligned:
            out_gather.pass_on()
        q, k = order(q, k)
        s = jnp.einsum("rthd,rjd->rhtj", q, k, preferred_element_type=F32) * HD**-0.5
        s = jnp.where(allowed[:, None], s, -1e30)
        p = jnp.exp(s - jnp.max(s, axis=-1, keepdims=True))
        p = p / jnp.sum(p, axis=-1, keepdims=True)
        if aligned:
            p, pieces, cot_z, down_gather.pieces = lax.optimization_barrier(
                (p, out_gather.pieces, cot_z, down_gather.pieces)
            )
            w_out = pieces
        pb = p.astype(BF)
        o = jnp.einsum("rhtj,rjd->rthd", pb, v, preferred_element_type=F32)
        o = o.astype(BF).reshape(2 * T, DH)
        o_w = order(o)
        away = swap_core(mm_pieces(o_w[T:], w_out))
        mid = x + bo + mm_pieces(o_w[:T], w_out) + away

        xhat2, rstd2 = ln_stats(mid)
        h2 = turn((xhat2 * g2 + b2).astype(BF), me)
        h2_z = gather(h2, "ctx").reshape(Z * T, D)

        order.mark(h2)
        up_gather = ChipGather(order(w_up.reshape(C * Z * R, F)), square)
        half = Z * T
        cot_z, down_pieces = order(cot_z, down_gather.pieces)
        cots = [cot_z, swap_core(cot_z)]
        if square:
            w_down = jnp.zeros((F, D), BF)
            places = [(0, 0), (1, 0), (2, 0), (3, 0), (3, 1)]
            for part, (block, j) in zip(down_pieces, places):
                at = (me ^ block) * F0 + j * (F0 // 2)
                w_down = lax.dynamic_update_slice_in_dim(w_down, part, at, 0)
        else:
            w_down = jnp.concatenate(down_pieces)
        order.mark(w_down)
        up_gather.pass_on()
        dacts = [side(part, w_down, 1, 1) for part in cots]
        w_up = jnp.concatenate(after(up_gather.pieces, dacts))
        order.mark(dacts, w_up)
        h2_z = order(h2_z)
        h2_mate = swap_core(h2_z)
        act, dpre = hidden(h2_z, w_up, bu, dacts[0])
        h2_mate, act, dpre = lax.optimization_barrier((h2_mate, act, dpre))
        h2s, acts, dpres = [h2_z, h2_mate], [act], [dpre]
        act, dpre = hidden(h2_mate, w_up, bu, dacts[1])
        acts.append(act)
        dpres.append(dpre)
        away = swap_core(near_nt(dpres[1], w_up, BF))
        dh2_part, away = lax.optimization_barrier((near_nt(dpres[0], w_up, F32), away))
        dh2_part = (dh2_part + away.astype(F32)).astype(BF).reshape(Z, T, D)
        order.mark(dh2_part)
        dh2 = turn(scatter(dh2_part, "ctx").astype(F32), me)
        dpre_w, act_w, h2_all, cot_all = (jnp.concatenate(order(*pair)) for pair in (dpres, acts, h2s, cots))

        def down_term(*parts, free=False):
            half = F0 // 2
            cols = [
                lax.dynamic_slice_in_dim(act_w, (me ^ i if square else i) * F0 + j * half, half, axis=1)
                for i, j in parts
            ]
            cols = jnp.concatenate(cols, axis=1)
            return side(cols, cot_all, 0, 0) if free else mm_tn(cols, cot_all)

        down_sum = ChipSum(down_term, square, AB)
        order.mark(down_sum.sent)
        up_sum = ChipSum(product(order(h2_all), dpre_w), square, AB)
        out_away = swap_core(mm(order(acts[1]), w_down).astype(BF))
        order.mark(up_sum.sent, out_away)
        down_sum.pass_on(order)
        order.mark(down_sum.sent)
        dh2 = order(dh2)
        order.mark(dh2)
        dmid = cotangent[0].astype(F32) + ln_back(dh2, g2, xhat2, rstd2)
        db = dmid.astype(BF)
        db = jnp.concatenate([db, swap_core(db)])
        do = mm_nt_pieces(db, w_out, BF)
        order.mark(do)
        do_h = order(do).reshape(2, T, HH, HD)
        dp = jnp.einsum("rthd,rjd->rhtj", do_h, v, preferred_element_type=F32)
        ds = (p * (dp - jnp.sum(p * dp, axis=-1, keepdims=True))).astype(BF)
        order.mark(ds, down_sum.far)
        ds = order(ds)
        dk = jnp.einsum("rhtj,rthd->rjd", ds, q, preferred_element_type=F32) * HD**-0.5
        dv = jnp.einsum("rhtj,rthd->rjd", pb, do_h, preferred_element_type=F32)
        dkv_away = swap_core(jnp.where(c == 0, dv, dk).astype(BF))
        dkv = jnp.where(c == 0, dk, dv) + dkv_away[::-1].astype(F32)
        dkv = dkv.astype(BF).reshape(2, Z, T, HD).transpose(1, 0, 2, 3)
        order.mark(dkv)
        dkv = lax.all_to_all(dkv, "ctx", 0, 0, tiled=True)
        mlp, out_away = lax.optimization_barrier((side(order(acts[0]), w_down, 1, 0), out_away))
        mlp = (mlp + out_away.astype(F32)).astype(BF).reshape(Z, T, D)
        order.mark(mlp)
        mlp = scatter(mlp, "ctx")
        ds_w = order(ds)
        dq = jnp.einsum("rhtj,rjd->rthd", ds_w, k, preferred_element_type=F32) * HD**-0.5
        dq = dq.astype(BF).reshape(2 * T, DH)
        if aligned:
            dq = turn(dq, me)
        order.mark(dq)
        dkv = order(dkv)
        dkv = jnp.sum(dkv.astype(F32), axis=0).astype(BF).reshape(2 * T, HD)
        dq_ext = jnp.concatenate([dq, dkv], axis=1)
        ext_sum = ChipSum(product(h1, dq_ext), square, AB)
        order.mark(ext_sum.sent)

        dq_w = order(dq_ext)
        dh1_away = swap_core(side(dq_w[T:], w_ext, 1, 1))
        dh1 = turn(side(dq_w[:T], w_ext, 1, 1) + dh1_away, me)
        up_sum.pass_on(order)
        order.mark(up_sum.sent, dh1)
        ext_sum.pass_on(order)
        order.mark(ext_sum.sent)
        if aligned:
            out_sum = ChipSum(product(o, order(db), side), square, AB, ext_sum.far)
            order.mark(out_sum.sent)
        dx = (dmid + ln_back(dh1, g1, xhat1, rstd1)).astype(BF)
        result = (mid + mlp.astype(F32) + bd).astype(BF)
        ext_sum.far, dx, result = lax.optimization_barrier((ext_sum.far, dx, result))
        g_ext = ext_sum.finish(order).astype(BF).reshape(2, Z, R, E)
        g_ext = g_ext.transpose(1, 0, 2, 3).reshape(Z, 2 * R, E)
        order.mark(g_ext)
        g_ext = scatter(g_ext, "ctx").reshape(2, R, E)
        g_up = up_sum.finish(order).astype(BF).reshape(C * Z, R, F)
        order.mark(g_up)
        g_up = lax.all_to_all(g_up, ("core", "ctx"), 0, 0, tiled=True)
        first, second = g_ext[0], g_ext[1]
        mate = swap_core(jnp.where(c == 0, second, first))
        mine = jnp.where(c == 0, first, second)
        first, second = jnp.where(c == 0, mine, mate), jnp.where(c == 0, mate, mine)
        g_q = [h[:, g * W0 : (g + 1) * W0] for g in range(G) for h in (first, second)]
        g_q = jnp.concatenate(g_q, axis=1).astype(F32)
        g_kv = jnp.concatenate([first[:, DH:], second[:, DH:]], axis=1).astype(F32)
        g_down = down_sum.finish(order, free=True)
        if aligned:
            if square:
                out_sum.near, g_down = lax.optimization_barrier((out_sum.near, g_down))
            out_sum.pass_on(order)
            order.mark(out_sum.sent)
            if square:
                out_sum.far, g_q, g_kv = lax.optimization_barrier((out_sum.far, g_q, g_kv))
            g_out = out_sum.finish(order).astype(BF).reshape(Z, R, D)
            order.mark(g_out)
            g_out = scatter(g_out, "ctx").astype(F32)
        else:
            g_out = mm_tn(o, order(db)).astype(BF)
            full = jnp.where(lax.broadcasted_iota(jnp.int32, (2, 1, 1), 0) == c, g_out[None], 0)
            g_out = scatter(full.reshape(N, R, D), EVERY).astype(F32)
        own_core = (lax.broadcasted_iota(jnp.int32, (1, 2, 1), 1) == c).astype(F32)
        own_cz = (lax.broadcasted_iota(jnp.int32, (1, C * Z, 1), 1) == c * Z + z).astype(F32)
        dh2_late, dpre_late, cot_late, dq_late, db_late = order(dh2, dpre_w, cotangent[0], dq_ext, db[:T])
        gb_up = jnp.sum(dpre_late.astype(F32), axis=0)
        gb_ext = jnp.sum(dq_late.astype(F32), axis=0)
        wide = [
            jnp.sum(dh1 * xhat1, axis=0),
            jnp.sum(dh1, axis=0),
            (gb_ext[:DH].reshape(G, 1, W0) * own_core).reshape(D),
            jnp.sum(db_late.astype(F32), axis=0),
            jnp.sum(dh2_late * xhat2, axis=0),
            jnp.sum(dh2_late, axis=0),
            jnp.sum(cot_late.astype(F32), axis=0),
        ]
        packed = jnp.concatenate(
            [w.reshape(N, R) for w in wide]
            + [
                (gb_up.reshape(AB, 1, F0) * own_cz).reshape(N, F0),
                jnp.where(c == 1, gb_ext[DH:], 0.0).reshape(N, vb0),
            ],
            axis=1,
        )
        packed = jnp.sum(lax.all_to_all(packed, EVERY, 0, 0, tiled=True), axis=0)
        g_up = g_up.reshape(C * Z, R, AB, F0).transpose(1, 2, 0, 3).reshape(R, FF).astype(F32)

        vecs = [packed[i * R : (i + 1) * R] for i in range(7)]
        gb_up = packed[7 * R : 7 * R + F0]
        gb_v = packed[7 * R + F0 :]
        return (
            result[None], dx[None],
            vecs[0], vecs[1], g_q, vecs[2], g_kv, gb_v, g_out, vecs[3],
            vecs[4], vecs[5], g_up, gb_up, g_down, vecs[6],
        )

    return local


def solution(mesh):
    dp, ctx = mesh.shape["dp"], mesh.shape["ctx"]
    chips = dp // 2
    a = next(i for i in range(int(chips**0.5), 0, -1) if chips % i == 0)
    b = chips // a
    fine = Mesh(mesh.devices.reshape(a, b, 2, ctx), EVERY)
    tok = P(("a", "b", "core"), "ctx", None)
    vec = P(EVERY)
    mat = P(EVERY, None)
    in_specs = (
        tok, P(("a", "b", "core"), None),
        vec, vec, mat, vec, mat, vec, mat, vec, vec, vec, mat, vec, mat, vec, tok,
    )
    out_specs = (tok, tok, vec, vec, mat, vec, mat, vec, mat, vec, vec, vec, mat, vec, mat, vec)
    return jax.shard_map(
        make_local(a, b, ctx), mesh=fine, in_specs=in_specs, out_specs=out_specs, check_vma=False
    )
```

```python
import jax
import jax.numpy as jnp
from jax import lax
from jax.experimental import pallas as pl
from jax.experimental.pallas import tpu as pltpu
from jax.sharding import Mesh, PartitionSpec as P

HEADS = 16
HD = 128
EPS = 1e-05
GELU_K = 0.7978845608028654
GELU_C = 0.044715

BF = jnp.bfloat16
F32 = jnp.float32
CHIP = ("a", "b")
EVERY = ("a", "b", "core", "ctx")
MATES = [(0, 1), (1, 0)]


def dot(a, b, dims):
    return lax.dot_general(a, b, (dims, ((), ())), preferred_element_type=F32)


def mm(a, b):
    return dot(a, b, ((1,), (0,)))


def mm_nt(a, b):
    return dot(a, b, ((1,), (1,)))


def mm_tn(a, b):
    return dot(a, b, ((0,), (0,)))


def side(a, b, ca, cb, out=F32):
    count, cols, depth = a.shape[1 - ca], b.shape[1 - cb], a.shape[ca]
    tile = next((t for t in (512, 384, 256, 128) if cols % t == 0), cols)

    def kernel(a_ref, b_ref, o_ref):
        o_ref[...] = lax.dot_general(
            a_ref[...], b_ref[...], (((ca,), (cb,)), ((), ())), preferred_element_type=F32
        ).astype(out)

    return pl.pallas_call(
        kernel,
        out_shape=jax.ShapeDtypeStruct((count, cols), out),
        grid=(cols // tile,),
        in_specs=[
            pl.BlockSpec(a.shape, lambda j: (0, 0)),
            pl.BlockSpec((depth, tile), lambda j: (0, j)) if cb == 0 else pl.BlockSpec((tile, depth), lambda j: (j, 0)),
        ],
        out_specs=pl.BlockSpec((count, tile), lambda j: (0, j)),
        compiler_params=pltpu.CompilerParams(vmem_limit_bytes=24 << 20),
        cost_estimate=pl.CostEstimate(flops=0, bytes_accessed=0, transcendentals=0),
        name="side",
    )(a, b)


def tile_of(cols, largest):
    return next((t for t in (512, 384, 256, 128) if t <= largest and cols % t == 0), cols)


def against(x, refs):
    total, at = None, 0
    for ref in refs:
        depth = ref.shape[0]
        part = jnp.dot(x[:, at : at + depth], ref[...], preferred_element_type=F32)
        total, at = part if total is None else total + part, at + depth
    return total


def cost(count, depth, cols, special=0):
    return pl.CostEstimate(
        flops=2 * count * depth * cols, bytes_accessed=2 * (count + cols) * depth, transcendentals=special
    )


def mm_pieces(x, pieces, bias=None, out=F32):
    count, depth = x.shape
    cols = pieces[0].shape[1]
    tile = tile_of(cols, 512)
    bias = jnp.zeros((cols,), F32) if bias is None else bias

    def kernel(x_ref, b_ref, *refs):
        refs[-1][...] = (against(x_ref, refs[:-1]) + b_ref[...]).astype(out)

    return pl.pallas_call(
        kernel,
        out_shape=jax.ShapeDtypeStruct((count, cols), out),
        grid=(cols // tile,),
        in_specs=[pl.BlockSpec((count, depth), lambda j: (0, 0)), pl.BlockSpec((1, tile), lambda j: (0, j))]
        + [pl.BlockSpec((p.shape[0], tile), lambda j: (0, j)) for p in pieces],
        out_specs=pl.BlockSpec((count, tile), lambda j: (0, j)),
        compiler_params=pltpu.CompilerParams(vmem_limit_bytes=24 << 20),
        cost_estimate=cost(count, depth, cols),
        name="rows_product",
    )(x, bias.reshape(1, cols), *pieces)


def mm_nt_pieces(x, pieces, out=F32):
    count, depth = x.shape
    cols = sum(p.shape[0] for p in pieces)

    def kernel(x_ref, *refs):
        at = 0
        for ref in refs[:-1]:
            part = lax.dot_general(x_ref[...], ref[...], (((1,), (1,)), ((), ())), preferred_element_type=F32)
            refs[-1][:, at : at + ref.shape[0]] = part.astype(out)
            at += ref.shape[0]

    return pl.pallas_call(
        kernel,
        out_shape=jax.ShapeDtypeStruct((count, cols), out),
        compiler_params=pltpu.CompilerParams(vmem_limit_bytes=32 << 20),
        cost_estimate=cost(count, depth, cols),
        name="columns_product",
    )(x, *pieces)


def hidden(h, w_up, bias, dact):
    count, depth = h.shape
    units = w_up.shape[1]
    tile = tile_of(units, 256)

    def kernel(h_ref, w_ref, b_ref, d_ref, act_ref, dpre_ref):
        @pl.loop(0, units // tile)
        def _(step):
            at = pl.ds(pl.multiple_of(step * tile, tile), tile)
            pre = jnp.dot(h_ref[...], w_ref[:, at], preferred_element_type=F32) + b_ref[:, at]
            square = pre * pre
            th = jnp.tanh(GELU_K * pre * (1.0 + GELU_C * square))
            half = 0.5 * (1.0 + th)
            act_ref[:, at] = (pre * half).astype(BF)
            slope = half + 0.5 * GELU_K * pre * (1.0 - th * th) * (1.0 + 3.0 * GELU_C * square)
            dpre_ref[:, at] = (d_ref[:, at] * slope).astype(BF)

    near = pl.BlockSpec(memory_space=pltpu.VMEM)
    return pl.pallas_call(
        kernel,
        out_shape=[jax.ShapeDtypeStruct((count, units), BF)] * 2,
        in_specs=[near] * 4,
        out_specs=[near] * 2,
        compiler_params=pltpu.CompilerParams(vmem_limit_bytes=16 << 20),
        cost_estimate=cost(count, depth, units, count * units),
        name="hidden",
    )(h, w_up, bias.reshape(1, units), dact)


def near_nt(x, w, out):
    count, depth = x.shape
    cols = w.shape[0]
    tile = tile_of(cols, 512)

    def kernel(x_ref, w_ref, o_ref):
        @pl.loop(0, cols // tile)
        def _(step):
            at = pl.ds(pl.multiple_of(step * tile, tile), tile)
            o_ref[:, at] = lax.dot_general(
                x_ref[...], w_ref[at, :], (((1,), (1,)), ((), ())), preferred_element_type=F32
            ).astype(out)

    near = pl.BlockSpec(memory_space=pltpu.VMEM)
    return pl.pallas_call(
        kernel,
        out_shape=jax.ShapeDtypeStruct((count, cols), out),
        in_specs=[near] * 2,
        out_specs=near,
        compiler_params=pltpu.CompilerParams(vmem_limit_bytes=16 << 20),
        cost_estimate=cost(count, depth, cols),
        name="near_product",
    )(x, w)


def ln_stats(x):
    mean = jnp.mean(x, axis=-1, keepdims=True)
    cen = x - mean
    var = jnp.mean(cen * cen, axis=-1, keepdims=True)
    rstd = lax.rsqrt(var + EPS)
    return cen * rstd, rstd


def ln_back(dh, gain, xhat, rstd):
    e = dh * gain
    me = jnp.mean(e, axis=-1, keepdims=True)
    mx = jnp.mean(e * xhat, axis=-1, keepdims=True)
    return (e - me - xhat * mx) * rstd


def after(x, *others):
    return lax.optimization_barrier((x, others))[0]


def swap_core(x):
    return lax.ppermute(x, "core", MATES)


def over_a(x):
    return lax.ppermute(x, "a", MATES)


def over_b(x):
    return lax.ppermute(x, "b", MATES)


def gather(x, axes):
    return lax.all_gather(x, axes, axis=0, tiled=False)


def scatter(x, axes):
    return lax.psum_scatter(x, axes, scatter_dimension=0, tiled=False)


class Order:
    def __init__(self):
        self.last = []

    def mark(self, *done):
        self.last = list(done)

    def __call__(self, *xs):
        xs = lax.optimization_barrier((xs, self.last))[0]
        return xs[0] if len(xs) == 1 else xs


class ChipGather:
    def __init__(self, x, square):
        self.square = square
        if not square:
            self.pieces = list(gather(x, CHIP).reshape((-1,) + x.shape))
            return
        self.pieces = [x, over_b(x), over_a(x)]

    def pass_on(self, *joint):
        if self.square:
            x, x1, x2 = self.pieces
            (x1, x2), joint = lax.optimization_barrier(((x1, x2), joint))
            half = x.shape[0] // 2
            self.pieces = [x, x1, x2, over_a(x1[:half]), over_b(x2[half:])]
        return joint


class ChipSum:
    def __init__(self, term, square, count, gate=()):
        self.square, self.term = square, term
        self.far = []
        if not square:
            full = jnp.stack([term((i, 0), (i, 1)) for i in range(count)])
            self.result = scatter(full.astype(BF), CHIP).astype(F32)
            self.sent = [full]
            return
        u = term((3, 0), (1, 0)).astype(BF)
        w = term((3, 1), (2, 1)).astype(BF)
        self.sent = [u, w]
        if gate:
            u, w = after((u, w), *gate)
        self.near = [over_b(u), over_a(w)]

    def pass_on(self, order):
        if self.square:
            u, w = self.near = order(*self.near)
            half = u.shape[0] // 2
            u = (self.term((2, 0)) + u[:half].astype(F32)).astype(BF)
            w = (self.term((1, 1)) + w[:half].astype(F32)).astype(BF)
            self.sent = [u, w]
            self.far = [over_a(u), over_b(w)]

    def finish(self, order, free=False):
        if not self.square:
            return self.result
        f0, f1 = order(*self.far)
        half = f0.shape[0]
        n0, n1 = self.near[0][half:], self.near[1][half:]
        return self.term((0, 0), (0, 1), free=free) + (
            jnp.concatenate([n0, n1]).astype(F32) + jnp.concatenate([f0, f1]).astype(F32)
        )


def make_local(A, B, Z):
    C = 2
    AB = A * B
    N = AB * C * Z
    square = A == 2 and B == 2

    def turn(x, me):
        if not square:
            return x
        w = x.shape[1] // AB
        cols = [x[:, i * w : (i + 1) * w] for i in range(AB)]
        return jnp.concatenate([lax.select_n(me ^ i, *cols) for i in range(AB)], axis=1)

    def product(left, right, multiply=None):
        half = left.shape[1] // AB // 2

        def term(*parts, free=False):
            cols = [left[:, (2 * i + j) * half : (2 * i + j + 1) * half] for i, j in parts]
            cols = jnp.concatenate(cols, axis=1)
            return side(cols, right, 0, 0) if free or multiply is not None else mm_tn(cols, right)

        return term

    def local(
        activations, segment_ids,
        ln1_gain, ln1_bias, q_weight, q_bias, kv_weight, v_bias, out_weight, out_bias,
        ln2_gain, ln2_bias, up_weight, up_bias, down_weight, down_bias, cotangent,
    ):
        T, D = activations.shape[1:]
        S = segment_ids.shape[1]
        R = q_weight.shape[0]
        F0 = down_weight.shape[0]
        F = AB * F0
        FF = up_weight.shape[1]
        DH = D // 2
        HH = HEADS // 2
        aligned = (Z * R) % HD == 0
        G = AB if aligned else 1
        W0 = DH // G
        E = DH + HD
        c = lax.axis_index("core")
        z = lax.axis_index("ctx")
        me = lax.axis_index("a") * B + lax.axis_index("b")

        order = Order()

        def half_of(i):
            cols = [q_weight[:, (g * 2 + i) * W0 : (g * 2 + i + 1) * W0] for g in range(G)]
            return jnp.concatenate(cols + [kv_weight[:, i * HD : (i + 1) * HD]], axis=1)

        first, second = half_of(0), half_of(1)
        mine = jnp.where(c == 0, first, second)
        mate = swap_core(jnp.where(c == 0, second, first))
        w_ext = jnp.concatenate([jnp.where(c == 0, mine, mate), jnp.where(c == 0, mate, mine)])
        order.mark(w_ext)
        w_ext_z = gather(w_ext, "ctx").reshape(Z, 2, R, E).transpose(1, 0, 2, 3).reshape(2 * Z * R, E)

        down_gather = ChipGather(order(down_weight), square)
        order.mark(w_ext)
        small, xin = order(
            [ln1_gain, ln1_bias, q_bias, out_bias, ln2_gain, ln2_bias, down_bias, up_bias, v_bias], activations[0]
        )
        vb0 = v_bias.shape[0]
        small = jnp.concatenate(small)
        small = jnp.broadcast_to(small[None], (N, small.shape[0]))
        small = lax.all_to_all(small, EVERY, 0, 0, tiled=True).astype(F32)
        g1, b1, bq, bo, g2, b2, bd = (small[:, i * R : (i + 1) * R].reshape(D) for i in range(7))
        bu = small[:, 7 * R : 7 * R + F0].reshape(AB, C * Z, F0)
        bu = lax.dynamic_index_in_dim(bu, c * Z + z, 1, keepdims=False).reshape(F)
        bv = small[:, 7 * R + F0 :].reshape(HD)
        bq = lax.dynamic_index_in_dim(bq.reshape(G, 2, W0), c, 1, keepdims=False).reshape(DH)
        b_ext = jnp.concatenate([bq, jnp.where(c == 1, bv, 0.0)])
        x = xin.astype(F32)
        xhat1, rstd1 = ln_stats(x)
        h1 = turn((xhat1 * g1 + b1).astype(BF), me)
        h1 = jnp.concatenate([h1, swap_core(h1)])
        seg = jnp.concatenate([segment_ids, swap_core(segment_ids)])
        start = z * T
        seg_q = lax.dynamic_slice_in_dim(seg, start, T, axis=1)
        q_at = start + jnp.arange(T, dtype=jnp.int32)
        k_at = jnp.arange(S, dtype=jnp.int32)
        allowed = (k_at[None, None, :] <= q_at[None, :, None]) & (seg[:, None, :] == seg_q[:, :, None])
        out_in = after(out_weight, w_ext_z)
        up_in = after(up_weight, w_ext_z)
        w_ext_z = order(w_ext_z)
        ext_gather = ChipGather(w_ext_z, square)
        if aligned:
            w_out_z = gather(out_in, "ctx").reshape(Z * R, D)
        else:
            w_out = gather(out_in, EVERY).reshape(2, DH, D)
            w_out_z = lax.dynamic_index_in_dim(w_out, c, 0, keepdims=False)
            w_out = [w_out_z]
        up_cols = [
            jnp.concatenate([up_in[:, (i * C * Z + j) * F0 : (i * C * Z + j + 1) * F0] for i in range(AB)], axis=1)
            for j in range(C * Z)
        ]
        w_up = lax.all_to_all(jnp.stack(up_cols), ("core", "ctx"), 0, 0, tiled=True)
        w_out_z, down_gather.pieces = ext_gather.pass_on(w_out_z, down_gather.pieces)
        down_gather.pass_on()
        ext_gather.pieces, w_up = lax.optimization_barrier((ext_gather.pieces, w_up))

        w_ext = jnp.concatenate(ext_gather.pieces)
        order.mark(w_ext)
        h1 = order(h1)
        if aligned:
            out_gather = ChipGather(w_out_z, square)
        cot_z = gather(after(cotangent[0], w_out_z), "ctx").reshape(Z * T, D)
        q_ext = mm_pieces(h1, ext_gather.pieces, b_ext, BF)
        kv = gather(q_ext[:, DH:].reshape(2, T, HD), "ctx").transpose(1, 0, 2, 3).reshape(2, S, HD)
        q = q_ext[:, :DH]
        if aligned:
            q = turn(q, me)
        q = q.reshape(2, T, HH, HD)
        kv_mate = swap_core(kv)[::-1]
        k = jnp.where(c == 0, kv, kv_mate)
        v = jnp.where(c == 0, kv_mate, kv)
        order.mark(kv)
        if aligned:
            out_gather.pass_on()
        q, k = order(q, k)
        s = jnp.einsum("rthd,rjd->rhtj", q, k, preferred_element_type=F32) * HD**-0.5
        s = jnp.where(allowed[:, None], s, -1e30)
        p = jnp.exp(s - jnp.max(s, axis=-1, keepdims=True))
        p = p / jnp.sum(p, axis=-1, keepdims=True)
        if aligned:
            p, pieces, cot_z, down_gather.pieces = lax.optimization_barrier(
                (p, out_gather.pieces, cot_z, down_gather.pieces)
            )
            w_out = pieces
        pb = p.astype(BF)
        o = jnp.einsum("rhtj,rjd->rthd", pb, v, preferred_element_type=F32)
        o = o.astype(BF).reshape(2 * T, DH)
        o_w = order(o)
        away = swap_core(mm_pieces(o_w[T:], w_out))
        mid = x + bo + mm_pieces(o_w[:T], w_out) + away

        xhat2, rstd2 = ln_stats(mid)
        h2 = turn((xhat2 * g2 + b2).astype(BF), me)
        h2_z = gather(h2, "ctx").reshape(Z * T, D)

        order.mark(h2)
        up_gather = ChipGather(order(w_up.reshape(C * Z * R, F)), square)
        half = Z * T
        cot_z, down_pieces = order(cot_z, down_gather.pieces)
        cots = [cot_z, swap_core(cot_z)]
        if square:
            w_down = jnp.zeros((F, D), BF)
            places = [(0, 0), (1, 0), (2, 0), (3, 0), (3, 1)]
            for part, (block, j) in zip(down_pieces, places):
                at = (me ^ block) * F0 + j * (F0 // 2)
                w_down = lax.dynamic_update_slice_in_dim(w_down, part, at, 0)
        else:
            w_down = jnp.concatenate(down_pieces)
        order.mark(w_down)
        up_gather.pass_on()
        dacts = [side(part, w_down, 1, 1) for part in cots]
        w_up = jnp.concatenate(after(up_gather.pieces, dacts))
        order.mark(dacts, w_up)
        h2_z = order(h2_z)
        h2_mate = swap_core(h2_z)
        act, dpre = hidden(h2_z, w_up, bu, dacts[0])
        h2_mate, act, dpre = lax.optimization_barrier((h2_mate, act, dpre))
        h2s, acts, dpres = [h2_z, h2_mate], [act], [dpre]
        act, dpre = hidden(h2_mate, w_up, bu, dacts[1])
        acts.append(act)
        dpres.append(dpre)
        away = swap_core(near_nt(dpres[1], w_up, BF))
        dh2_part, away = lax.optimization_barrier((near_nt(dpres[0], w_up, F32), away))
        dh2_part = (dh2_part + away.astype(F32)).astype(BF).reshape(Z, T, D)
        order.mark(dh2_part)
        dh2 = turn(scatter(dh2_part, "ctx").astype(F32), me)
        dpre_w, act_w, h2_all, cot_all = (jnp.concatenate(order(*pair)) for pair in (dpres, acts, h2s, cots))

        def down_term(*parts, free=False):
            half = F0 // 2
            cols = [
                lax.dynamic_slice_in_dim(act_w, (me ^ i if square else i) * F0 + j * half, half, axis=1)
                for i, j in parts
            ]
            cols = jnp.concatenate(cols, axis=1)
            return side(cols, cot_all, 0, 0) if free else mm_tn(cols, cot_all)

        down_sum = ChipSum(down_term, square, AB)
        order.mark(down_sum.sent)
        up_sum = ChipSum(product(order(h2_all), dpre_w), square, AB)
        out_away = swap_core(mm(order(acts[1]), w_down).astype(BF))
        order.mark(up_sum.sent, out_away)
        down_sum.pass_on(order)
        order.mark(down_sum.sent)
        dh2 = order(dh2)
        order.mark(dh2)
        dmid = cotangent[0].astype(F32) + ln_back(dh2, g2, xhat2, rstd2)
        db = dmid.astype(BF)
        db = jnp.concatenate([db, swap_core(db)])
        do = mm_nt_pieces(db, w_out, BF)
        order.mark(do)
        do_h = order(do).reshape(2, T, HH, HD)
        dp = jnp.einsum("rthd,rjd->rhtj", do_h, v, preferred_element_type=F32)
        ds = (p * (dp - jnp.sum(p * dp, axis=-1, keepdims=True))).astype(BF)
        order.mark(ds, down_sum.far)
        ds = order(ds)
        dk = jnp.einsum("rhtj,rthd->rjd", ds, q, preferred_element_type=F32) * HD**-0.5
        dv = jnp.einsum("rhtj,rthd->rjd", pb, do_h, preferred_element_type=F32)
        dkv_away = swap_core(jnp.where(c == 0, dv, dk).astype(BF))
        dkv = jnp.where(c == 0, dk, dv) + dkv_away[::-1].astype(F32)
        dkv = dkv.astype(BF).reshape(2, Z, T, HD).transpose(1, 0, 2, 3)
        order.mark(dkv)
        dkv = lax.all_to_all(dkv, "ctx", 0, 0, tiled=True)
        mlp, out_away = lax.optimization_barrier((side(order(acts[0]), w_down, 1, 0), out_away))
        mlp = (mlp + out_away.astype(F32)).astype(BF).reshape(Z, T, D)
        order.mark(mlp)
        mlp = scatter(mlp, "ctx")
        ds_w = order(ds)
        dq = jnp.einsum("rhtj,rjd->rthd", ds_w, k, preferred_element_type=F32) * HD**-0.5
        dq = dq.astype(BF).reshape(2 * T, DH)
        if aligned:
            dq = turn(dq, me)
        order.mark(dq)
        dkv = order(dkv)
        dkv = jnp.sum(dkv.astype(F32), axis=0).astype(BF).reshape(2 * T, HD)
        dq_ext = jnp.concatenate([dq, dkv], axis=1)
        ext_sum = ChipSum(product(h1, dq_ext), square, AB)
        order.mark(ext_sum.sent)

        if square:
            up_sum.near, dq_w = lax.optimization_barrier((up_sum.near, dq_ext))
        else:
            dq_w = dq_ext
        dh1 = side(dq_w, w_ext, 1, 1)
        dh1 = turn(dh1[:T] + swap_core(dh1[T:]), me)
        up_sum.pass_on(order)
        order.mark(up_sum.sent, dh1)
        ext_sum.pass_on(order)
        order.mark(ext_sum.sent)
        if aligned:
            out_sum = ChipSum(product(o, order(db), side), square, AB, ext_sum.far)
            order.mark(out_sum.sent)
        dx = (dmid + ln_back(dh1, g1, xhat1, rstd1)).astype(BF)
        result = (mid + mlp.astype(F32) + bd).astype(BF)
        ext_sum.far, dx, result = lax.optimization_barrier((ext_sum.far, dx, result))
        g_ext = ext_sum.finish(order).astype(BF).reshape(2, Z, R, E)
        g_ext = g_ext.transpose(1, 0, 2, 3).reshape(Z, 2 * R, E)
        order.mark(g_ext)
        g_ext = scatter(g_ext, "ctx").reshape(2, R, E)
        g_up = up_sum.finish(order).astype(BF).reshape(C * Z, R, F)
        order.mark(g_up)
        g_up = lax.all_to_all(g_up, ("core", "ctx"), 0, 0, tiled=True)
        first, second = g_ext[0], g_ext[1]
        mate = swap_core(jnp.where(c == 0, second, first))
        mine = jnp.where(c == 0, first, second)
        first, second = jnp.where(c == 0, mine, mate), jnp.where(c == 0, mate, mine)
        g_q = [h[:, g * W0 : (g + 1) * W0] for g in range(G) for h in (first, second)]
        g_q = jnp.concatenate(g_q, axis=1).astype(F32)
        g_kv = jnp.concatenate([first[:, DH:], second[:, DH:]], axis=1).astype(F32)
        g_down = down_sum.finish(order, free=True)
        if aligned:
            if square:
                out_sum.near, g_down = lax.optimization_barrier((out_sum.near, g_down))
            out_sum.pass_on(order)
            order.mark(out_sum.sent)
            if square:
                out_sum.far, g_q, g_kv = lax.optimization_barrier((out_sum.far, g_q, g_kv))
            g_out = out_sum.finish(order).astype(BF).reshape(Z, R, D)
            order.mark(g_out)
            g_out = scatter(g_out, "ctx").astype(F32)
        else:
            g_out = mm_tn(o, order(db)).astype(BF)
            full = jnp.where(lax.broadcasted_iota(jnp.int32, (2, 1, 1), 0) == c, g_out[None], 0)
            g_out = scatter(full.reshape(N, R, D), EVERY).astype(F32)
        own_core = (lax.broadcasted_iota(jnp.int32, (1, 2, 1), 1) == c).astype(F32)
        own_cz = (lax.broadcasted_iota(jnp.int32, (1, C * Z, 1), 1) == c * Z + z).astype(F32)
        dh2_late, dpre_late, cot_late, dq_late, db_late = order(dh2, dpre_w, cotangent[0], dq_ext, db[:T])
        gb_up = jnp.sum(dpre_late.astype(F32), axis=0)
        gb_ext = jnp.sum(dq_late.astype(F32), axis=0)
        wide = [
            jnp.sum(dh1 * xhat1, axis=0),
            jnp.sum(dh1, axis=0),
            (gb_ext[:DH].reshape(G, 1, W0) * own_core).reshape(D),
            jnp.sum(db_late.astype(F32), axis=0),
            jnp.sum(dh2_late * xhat2, axis=0),
            jnp.sum(dh2_late, axis=0),
            jnp.sum(cot_late.astype(F32), axis=0),
        ]
        packed = jnp.concatenate(
            [w.reshape(N, R) for w in wide]
            + [
                (gb_up.reshape(AB, 1, F0) * own_cz).reshape(N, F0),
                jnp.where(c == 1, gb_ext[DH:], 0.0).reshape(N, vb0),
            ],
            axis=1,
        )
        packed = jnp.sum(lax.all_to_all(packed, EVERY, 0, 0, tiled=True), axis=0)
        g_up = g_up.reshape(C * Z, R, AB, F0).transpose(1, 2, 0, 3).reshape(R, FF).astype(F32)

        vecs = [packed[i * R : (i + 1) * R] for i in range(7)]
        gb_up = packed[7 * R : 7 * R + F0]
        gb_v = packed[7 * R + F0 :]
        return (
            result[None], dx[None],
            vecs[0], vecs[1], g_q, vecs[2], g_kv, gb_v, g_out, vecs[3],
            vecs[4], vecs[5], g_up, gb_up, g_down, vecs[6],
        )

    return local


def solution(mesh):
    dp, ctx = mesh.shape["dp"], mesh.shape["ctx"]
    chips = dp // 2
    a = next(i for i in range(int(chips**0.5), 0, -1) if chips % i == 0)
    b = chips // a
    fine = Mesh(mesh.devices.reshape(a, b, 2, ctx), EVERY)
    tok = P(("a", "b", "core"), "ctx", None)
    vec = P(EVERY)
    mat = P(EVERY, None)
    in_specs = (
        tok, P(("a", "b", "core"), None),
        vec, vec, mat, vec, mat, vec, mat, vec, vec, vec, mat, vec, mat, vec, tok,
    )
    out_specs = (tok, tok, vec, vec, mat, vec, mat, vec, mat, vec, vec, vec, mat, vec, mat, vec)
    return jax.shard_map(
        make_local(a, b, ctx), mesh=fine, in_specs=in_specs, out_specs=out_specs, check_vma=False
    )
```
